512 devices in a mesh: gr: 16 (over z_hi, y, core), gc: 32 (over x, z_lo).
Axes of the slice: x: 4, y: 4, z: 16 (z_hi: 2, z_lo: 8; z = z_hi * 8 + z_lo), core: 2. Of those that a mesh axis runs over, the one named last changes fastest.
Arguments:
- features: bfloat16 [65536, 1024], P(('gr', 'gc')), may hold values from -6 to 6
- weight: bfloat16 [1024, 1024], replicated, may hold values from -0.1875 to 0.1875
- cotangent: bfloat16 [65536, 1024], P(('gr', 'gc')), may hold values from -6 to 6
- block_values: bfloat16 [512, 16, 128, 128], P(('gr', 'gc')), as said below
- block_codes: int32 [512, 16], P(('gr', 'gc')), may hold values from 0 to 511, as said below
- block_count: int32 [512], P(('gr', 'gc')), may hold values from 1 to 16, as said below
Outputs:
- output: float32 [65536, 1024], P(('gr', 'gc'))
- input_grad: float32 [65536, 1024], P(('gr', 'gc'))
- weight_grad: float32 [1024, 1024], P('gc')
The draws below stay inside these ranges and needn't reach their ends.
Inputs may be any that keep to these rules, and one draw needn't show every extreme that they name: `block_codes`: write code = row * 512 + column. In every slot, row lies in 0 to 0 and column is a block of a slice s + j * 32 with |j| <= 8 (same grid column, at most 8 grid rows away). The codes of the live slots of one slice differ from one another. Every diagonal block (block row equal to block column) is live. The live slots of a slice are its first block_count slots; the entries of later slots are not part of the adjacency. In every draw some slice has all 16 slots live. `block_values`: the adjacency is symmetric: a block is live exactly when its mirror block is, and its entries are the transpose of the mirror's.
All inputs are finite; a program needn't handle non-finite values.
Results may differ from the reference program's by a relative error of at most 0.0045.
Values may be sent and summed in bfloat16 or wider, within the bound.
No kernel may reach another device: no remote copies, remote signals or barrier semaphores. Data moves between devices by JAX's collectives and lax.ppermute only.
A program may use at most 64 MiB of HBM per device.

```python
import jax
import jax.numpy as jnp
from jax import lax

F = 1024
BLK = 128
ROWS = 128
REACH = 8
ROWBLK = 1
MAXB = 16
SLICES = 512
NODES = 65536
NB = 512
N_GR = 16
N_GC = 32


def block_layout(key):
    slot_ids = jnp.arange(MAXB)
    row_in = slot_ids // (N_GR * ROWBLK)
    target_row = slot_ids // ROWBLK % N_GR
    col_in = slot_ids % ROWBLK
    slice_ids = jnp.arange(SLICES)[:, None]
    shift_rows = target_row[None, :] - slice_ids // N_GC
    inside = jnp.abs(shift_rows) <= REACH
    src_block = slice_ids * ROWBLK + row_in[None, :]
    dst_block = (slice_ids + shift_rows * N_GC) * ROWBLK + col_in[None, :]
    dst_block = jnp.where(inside, dst_block, src_block)
    low_block = jnp.minimum(src_block, dst_block)
    high_block = jnp.maximum(src_block, dst_block)
    pair_span = REACH * N_GC * ROWBLK + ROWBLK
    pair_ids = low_block * pair_span + (high_block - low_block)
    pair_draw = jax.random.randint(jax.random.fold_in(key, 11), (NB * pair_span,), 0, 100)
    chosen = pair_draw[pair_ids] < 60
    full_slice = REACH * N_GC
    touches = (slice_ids == full_slice) | (dst_block // ROWBLK == full_slice)
    active = inside & (chosen | (src_block == dst_block) | touches)
    slot_order = jnp.argsort(1 - active.astype(jnp.int32), axis=1, stable=True)
    codes = row_in[None, :] * NB + dst_block
    slot_codes = jnp.take_along_axis(codes, slot_order, axis=1).astype(jnp.int32)
    ordered_pairs = jnp.take_along_axis(pair_ids, slot_order, axis=1)
    flipped = jnp.take_along_axis(src_block > dst_block, slot_order, axis=1)
    diagonal = jnp.take_along_axis(src_block == dst_block, slot_order, axis=1)
    block_total = jnp.sum(active.astype(jnp.int32), axis=1).astype(jnp.int32)
    return (slot_codes, block_total, ordered_pairs, flipped, diagonal)


def draw_block_values(key, part):
    slot_codes, block_total, ordered_pairs, flipped, diagonal = block_layout(key)
    spread = (BLK * ROWBLK * (2 * REACH + 1) * 0.6) ** (-0.5)
    value_key = jax.random.fold_in(key, 23)

    def one_block(pair_id):
        sub_key = jax.random.fold_in(value_key, pair_id)
        return jax.random.normal(sub_key, (BLK, BLK), jnp.float32)
    base = jax.vmap(one_block)(ordered_pairs.reshape(-1)).reshape(SLICES, MAXB, BLK, BLK)
    turned = jnp.swapaxes(base, 2, 3)
    blocks = jnp.where(flipped[:, :, None, None], turned, base)
    blocks = jnp.where(diagonal[:, :, None, None], (base + turned) * 0.7071, blocks)
    return (blocks * spread).astype(jnp.bfloat16)


def draw_block_codes(key, part):
    return block_layout(key)[0]


def draw_block_count(key, part):
    return block_layout(key)[1]


def shard_levels(rng, dims, split, smallest, top_value):
    def one(dim, blocks):
        draws = jax.random.uniform(jax.random.fold_in(jax.random.fold_in(rng, 6), dim), (blocks,), jnp.float32, smallest / len(split), top_value / len(split))
        return jnp.repeat(jnp.exp(draws), dims[dim] // blocks).reshape((-1,) + (1,) * (len(dims) - dim - 1))

    loudness = one(*split[0])
    for cut in split[1:]:
        loudness = loudness * one(*cut)
    return loudness


def centred(own_key, shape, deviation, limit, pieces=(), dtype=jnp.bfloat16):
    values = jax.random.normal(own_key, shape, jnp.float32) * deviation
    if len(pieces) > 0:
        values = shard_levels(own_key, shape, pieces, -0.22, 0.18) * values
    return jnp.clip(values, min=-limit, max=limit).astype(dtype)


def setup_inputs(seed: int = 0) -> dict:
    streams_of = jax.random.split(jax.random.key(seed), 7)
    features = centred(streams_of[0], (NODES, F), 1.0, 6.0, ((0, 512),))
    weight = centred(streams_of[1], (F, F), F ** -0.5, 0.1875)
    cotangent = centred(streams_of[2], (NODES, F), 1.0, 6.0, ((0, 512),))
    block_values = draw_block_values(jax.random.fold_in(streams_of[6], 71), 0)
    block_codes = draw_block_codes(jax.random.fold_in(streams_of[6], 71), 0)
    block_count = draw_block_count(jax.random.fold_in(streams_of[6], 71), 0)
    return {"features": features, "weight": weight, "cotangent": cotangent, "block_values": block_values, "block_codes": block_codes, "block_count": block_count}


def reference(features, weight, cotangent, block_values, block_codes, block_count):
    projected = jnp.dot(features, weight, preferred_element_type=jnp.float32).astype(jnp.bfloat16)
    proj_blocks = projected.reshape(NB, BLK, F)
    slot_ids = jnp.arange(MAXB)
    row_choices = jnp.arange(ROWBLK)

    def forward_slice(slice_item):
        values, slot_codes, block_total = slice_item
        active = slot_ids < block_total
        row_index = slot_codes // NB
        column_block = slot_codes % NB
        gathered_rows = proj_blocks[column_block].astype(jnp.float32)
        products = jnp.einsum("kij,kjf->kif", values.astype(jnp.float32), gathered_rows)
        select_row = ((row_index[:, None] == row_choices[None, :]) & active[:, None]).astype(jnp.float32)
        return jnp.einsum("ka,kif->aif", select_row, products).reshape(ROWS, F)

    summed = lax.map(forward_slice, (block_values, block_codes, block_count)).reshape(NODES, F)
    sigmoid = jax.nn.sigmoid(summed)
    output = summed * sigmoid
    act_slope = (cotangent.astype(jnp.float32) * sigmoid * (1.0 + summed * (1.0 - sigmoid))).astype(jnp.bfloat16)
    slope_blocks = act_slope.reshape(SLICES, ROWBLK, BLK, F)

    def backward_slice(running, slice_item):
        values, slot_codes, block_total, slope_here = slice_item
        active = (slot_ids < block_total).astype(jnp.float32)
        row_index = slot_codes // NB
        column_block = slot_codes % NB
        source_rows = slope_here[row_index].astype(jnp.float32)
        products = jnp.einsum("kij,kif->kjf", values.astype(jnp.float32), source_rows) * active[:, None, None]
        return running.at[column_block].add(products), None

    grad_blocks, unused = lax.scan(backward_slice, jnp.zeros((NB, BLK, F), jnp.float32), (block_values, block_codes, block_count, slope_blocks))
    back_grad = grad_blocks.reshape(NODES, F).astype(jnp.bfloat16)
    input_grad = jnp.dot(back_grad, weight.T, preferred_element_type=jnp.float32)
    weight_grad = jnp.dot(features.T, back_grad, preferred_element_type=jnp.float32) * (NODES ** -0.5)
    return output, input_grad, weight_grad
```

```python
import jax
import jax.numpy as jnp
from jax import lax
from jax.experimental import pallas as pl
from jax.experimental.pallas import tpu as pltpu
from jax.sharding import Mesh, PartitionSpec as P

AXES = ("zh", "y", "co", "x", "zl")
SIZES = (2, 4, 2, 4, 8)
BF16, F32 = jnp.bfloat16, jnp.float32
SWAP = [(0, 1), (1, 0)]
VMEM = pl.BlockSpec(memory_space=pltpu.VMEM)


def dot(a, b):
    return jnp.dot(a, b, preferred_element_type=F32)


def call(body, outs, *args):
    return pl.pallas_call(
        body,
        out_shape=outs,
        in_specs=[VMEM] * len(args),
        out_specs=jax.tree.map(lambda _: VMEM, outs),
        compiler_params=pltpu.CompilerParams(vmem_limit_bytes=48 * 2**20),
    )(*args)


def forward_body(tile, near, far_same, far_other, weight, cotangent, out, slope, mixed):
    total = near[...]
    total += dot(tile[:, 1024:1536], far_same[...])
    total += dot(tile[:, 1536:2048], far_other[...])
    mixed_here = total.astype(BF16)
    mixed[...] = mixed_here
    summed = dot(mixed_here, weight[...])
    sigmoid = jax.nn.sigmoid(summed)
    out[...] = summed * sigmoid
    slope[...] = (
        cotangent[...].astype(F32) * sigmoid * (1.0 + summed * (1.0 - sigmoid))
    ).astype(BF16)


def backward_body(tile, near, far_same, far_other, weight, input_grad):
    total = near[...]
    total += dot(tile[:, 1024:1536], far_same[...])
    total += dot(tile[:, 1536:2048], far_other[...])
    input_grad[...] = lax.dot_general(
        total.astype(BF16), weight[...], (((1,), (1,)), ((), ())), preferred_element_type=F32
    )


def near_body(tile, near_same, near_other, near):
    near[...] = dot(tile[:, 0:512], near_same[...]) + dot(tile[:, 512:1024], near_other[...])


def partial_body(core, factors, near_same, near_other, partial):
    mine = core[0]
    total = jnp.zeros(partial.shape, F32)
    for y in range(4):
        rows = slice(128 * y, 128 * y + 128)
        total += dot(factors[2 * y + mine], near_same[rows, :])
        total += dot(factors[2 * y + 1 - mine], near_other[rows, :])
    partial[...] = total


def spread(rows, axes, count):
    return lax.all_to_all(jnp.broadcast_to(rows[None], (count,) + rows.shape), axes, 0, 0)


def over_y(rows):
    same = spread(rows, "y", 4).reshape(512, rows.shape[1])
    return same, lax.ppermute(same, "co", SWAP)


def local(features, weight, cotangent, block_values, block_codes, block_count):
    zh, core = lax.axis_index("zh"), lax.axis_index("co")
    hidden = features.shape[1]
    grid_row = block_codes[0] % 512 // 32
    place = (grid_row // 8 ^ zh) * 8 + (grid_row % 2 ^ core) * 4 + grid_row % 8 // 2
    active = jnp.arange(16) < block_count[0]
    select = (place[:, None] == jnp.arange(16)[None, :]) & active[:, None]
    tile = jnp.einsum("km,kij->imj", select.astype(BF16), block_values[0], preferred_element_type=F32)
    tile = tile.astype(BF16).reshape(128, 2048)
    at = jnp.arange(hidden)
    group, to_x, to_zh, to_zl, last = at // 128, at // 32 % 4, at // 16 % 2, at // 2 % 8, at % 2
    source = 32 * (8 * to_x + to_zl) + 16 * to_zh + 2 * group + last
    regroup = (source[:, None] == at[None, :]).astype(BF16)

    rows_f32 = jax.ShapeDtypeStruct(features.shape, F32)
    rows_bf16 = jax.ShapeDtypeStruct(features.shape, BF16)

    far = lax.ppermute(features, "zh", SWAP)
    near_same, near_other = over_y(features)
    near = call(near_body, rows_f32, tile, near_same, near_other)
    far_same, far_other = over_y(far)
    output, slope, mixed = call(
        forward_body, (rows_f32, rows_bf16, rows_bf16),
        tile, near, far_same, far_other, weight, cotangent,
    )

    far = lax.ppermute(slope, "zh", SWAP)
    near_same, near_other = over_y(slope)
    factors = lax.dot_general(
        regroup, mixed, (((1,), (1,)), ((), ())), preferred_element_type=F32
    ).astype(BF16)
    factors = lax.all_to_all(factors.reshape(8, 128, 128), ("y", "co"), 0, 0)
    partial = pl.pallas_call(
        partial_body,
        out_shape=jax.ShapeDtypeStruct((128, hidden), F32),
        in_specs=[pl.BlockSpec(memory_space=pltpu.SMEM), VMEM, VMEM, VMEM],
        out_specs=VMEM,
        compiler_params=pltpu.CompilerParams(vmem_limit_bytes=48 * 2**20),
    )(core.reshape(1), factors, near_same, near_other)
    near = call(near_body, rows_f32, tile, near_same, near_other)
    far_same, far_other = over_y(far)
    input_grad = call(backward_body, rows_f32, tile, near, far_same, far_other, weight)

    part = lax.all_to_all(partial.reshape(4, 32, hidden), "x", 0, 0).sum(0)
    part = lax.all_to_all(part.reshape(16, 2, hidden), ("zh", "zl"), 0, 0).sum(0)
    part = part * (65536 ** -0.5)
    weight_grad = spread(part, ("zh", "y", "co"), 16).reshape(32, hidden)
    return output, input_grad, weight_grad


def solution(mesh):
    fine = Mesh(mesh.devices.reshape(SIZES), AXES)
    rows = P(AXES)
    return jax.shard_map(
        local,
        mesh=fine,
        in_specs=(rows, P(), rows, rows, rows, rows),
        out_specs=(rows, rows, P(("x", "zl"))),
        check_vma=False,
    )
```

```python
import jax
import jax.numpy as jnp
from jax import lax
from jax.experimental import pallas as pl
from jax.experimental.pallas import tpu as pltpu
from jax.sharding import Mesh, PartitionSpec as P

AXES = ("zh", "y", "co", "x", "zl")
SIZES = (2, 4, 2, 4, 8)
BF16, F32 = jnp.bfloat16, jnp.float32
SWAP = [(0, 1), (1, 0)]
VMEM = pl.BlockSpec(memory_space=pltpu.VMEM)


def dot(a, b):
    return jnp.dot(a, b, preferred_element_type=F32)


def call(body, outs, *args):
    return pl.pallas_call(
        body,
        out_shape=outs,
        in_specs=[VMEM] * len(args),
        out_specs=jax.tree.map(lambda _: VMEM, outs),
        compiler_params=pltpu.CompilerParams(vmem_limit_bytes=48 * 2**20),
        cost_estimate=pl.CostEstimate(flops=1, bytes_accessed=1, transcendentals=0),
    )(*args)


def forward_body(tile, near, far_same, far_other, weight, cotangent, out, slope, mixed):
    total = near[...]
    total += dot(tile[:, 1024:1536], far_same[...])
    total += dot(tile[:, 1536:2048], far_other[...])
    mixed_here = total.astype(BF16)
    mixed[...] = mixed_here
    summed = dot(mixed_here, weight[...])
    sigmoid = jax.nn.sigmoid(summed)
    out[...] = summed * sigmoid
    slope[...] = (
        cotangent[...].astype(F32) * sigmoid * (1.0 + summed * (1.0 - sigmoid))
    ).astype(BF16)


def backward_body(near, far_first, far_last, weight, input_grad):
    far = jnp.concatenate([far_first[...], far_last[...]], axis=0)
    total = near[...] + far.astype(F32)
    input_grad[...] = lax.dot_general(
        total.astype(BF16), weight[...], (((1,), (1,)), ((), ())), preferred_element_type=F32
    )


def near_body(tile, near_same, near_other, near):
    near[...] = dot(tile[:, 0:512], near_same[...]) + dot(tile[:, 512:1024], near_other[...])


def partial_body(core, factors, near_same, near_other, partial):
    mine = core[0]
    total = jnp.zeros(partial.shape, F32)
    for y in range(4):
        rows = slice(128 * y, 128 * y + 128)
        total += dot(factors[2 * y + mine], near_same[rows, :])
        total += dot(factors[2 * y + 1 - mine], near_other[rows, :])
    partial[...] = total.astype(partial.dtype)


def grouped(core, factors, near_same, near_other, dtype):
    return pl.pallas_call(
        partial_body,
        out_shape=jax.ShapeDtypeStruct((128, near_same.shape[1]), dtype),
        in_specs=[pl.BlockSpec(memory_space=pltpu.SMEM), VMEM, VMEM, VMEM],
        out_specs=VMEM,
        compiler_params=pltpu.CompilerParams(vmem_limit_bytes=48 * 2**20),
        cost_estimate=pl.CostEstimate(flops=1, bytes_accessed=1, transcendentals=0),
    )(core, factors, near_same, near_other)


def along_z(rows, step):
    pairs = []
    for z in range(16):
        for core in range(2):
            to = (z + (step if core == 0 else -step)) % 16
            pairs.append((z // 8 * 16 + core * 8 + z % 8, to // 8 * 16 + core * 8 + to % 8))
    return lax.ppermute(rows, ("zh", "co", "zl"), pairs)


def after(value, *others):
    return lax.optimization_barrier((value,) + others)[0]


def spread(rows, axes, count):
    return lax.all_to_all(jnp.broadcast_to(rows[None], (count,) + rows.shape), axes, 0, 0)


def over_y(rows):
    return spread(rows, "y", 4).reshape(512, rows.shape[1])


def other_core(rows):
    return lax.ppermute(rows, "co", SWAP)


def local(features, weight, cotangent, block_values, block_codes, block_count):
    zh, core = lax.axis_index("zh"), lax.axis_index("co")
    hidden = features.shape[1]
    grid_row = block_codes[0] % 512 // 32
    place = (grid_row // 8 ^ zh) * 8 + (grid_row % 2 ^ core) * 4 + grid_row % 8 // 2
    active = jnp.arange(16) < block_count[0]
    other = (grid_row[:, None] == jnp.arange(8)[None, :] + 8 * (1 - zh)) & active[:, None]
    mirror = jnp.einsum("km,kij->mji", other.astype(BF16), block_values[0], preferred_element_type=F32)
    mirror = mirror.astype(BF16)
    select = (place[:, None] == jnp.arange(16)[None, :]) & active[:, None]
    tile = jnp.einsum("km,kij->imj", select.astype(BF16), block_values[0], preferred_element_type=F32)
    tile = tile.astype(BF16).reshape(128, 2048)
    at = jnp.arange(hidden)
    source = 32 * (at // 4 % 32) + 4 * (at // 128) + at % 4
    regroup = (source[:, None] == at[None, :]).astype(BF16)

    rows_f32 = jax.ShapeDtypeStruct(features.shape, F32)
    rows_bf16 = jax.ShapeDtypeStruct(features.shape, BF16)

    far = along_z(along_z(features, 1), 7)
    near_same = over_y(features)
    near_other = other_core(near_same)
    mirror = lax.all_to_all(after(mirror, near_same), ("y", "co"), 0, 0)
    near = call(near_body, rows_f32, tile, near_same, near_other)
    far_same = over_y(after(far, mirror))
    far_other = other_core(far_same)
    output, slope, mixed = call(
        forward_body, (rows_f32, rows_bf16, rows_bf16),
        tile, near, far_same, far_other, weight, cotangent,
    )

    factors = lax.dot_general(
        regroup, mixed, (((1,), (1,)), ((), ())), preferred_element_type=F32
    ).astype(BF16)
    factors = lax.all_to_all(factors.reshape(8, 128, 128), ("y", "co"), 0, 0)
    near_same = over_y(slope)
    near_other = other_core(after(near_same, factors))
    far = grouped(core.reshape(1), mirror, near_same, near_other, BF16)
    far = along_z(far, 1)
    half = far.shape[0] // 2
    far_first, far_last = along_z(far[:half], 7), along_z(far[half:], 7)
    partial = grouped(core.reshape(1), factors, near_same, near_other, BF16)
    near = call(near_body, rows_f32, tile, near_same, near_other)

    part = lax.all_to_all(after(partial, far).reshape(4, 32, hidden), "x", 0, 0)
    part = part.astype(F32).sum(0).astype(BF16).reshape(8, 4, hidden)
    part = jnp.concatenate([after(part, far_first)] * 2)
    part = lax.all_to_all(part, ("zh", "zl"), 0, 0)
    part = part.astype(F32).sum(0) * (65536 ** -0.5)
    weight_grad = spread(after(part, far_last), ("y", "co"), 8).reshape(32, hidden)
    input_grad = call(backward_body, rows_f32, near, far_first, far_last, weight)
    return output, input_grad, weight_grad


def solution(mesh):
    fine = Mesh(mesh.devices.reshape(SIZES), AXES)
    rows = P(AXES)
    return jax.shard_map(
        local,
        mesh=fine,
        in_specs=(rows, P(), rows, rows, rows, rows),
        out_specs=(rows, rows, P(("x", "zl"))),
        check_vma=False,
    )
```

```python
import jax
import jax.numpy as jnp
from jax import lax
from jax.experimental import pallas as pl
from jax.experimental.pallas import tpu as pltpu
from jax.sharding import Mesh, PartitionSpec as P

AXES = ("zh", "y", "co", "x", "zl")
SIZES = (2, 4, 2, 4, 8)
BF16, F32 = jnp.bfloat16, jnp.float32
SWAP = [(0, 1), (1, 0)]
VMEM = pl.BlockSpec(memory_space=pltpu.VMEM)
SMEM = pl.BlockSpec(memory_space=pltpu.SMEM)
COLS = slice(0, 1024)


def dot(a, b, over_a=1, over_b=0):
    return lax.dot_general(a, b, (((over_a,), (over_b,)), ((), ())), preferred_element_type=F32)


def call(body, outs, *args, flops=1):
    return pl.pallas_call(
        body,
        out_shape=outs,
        in_specs=[SMEM if a.shape == (1,) else VMEM for a in args],
        out_specs=jax.tree.map(lambda _: VMEM, outs),
        compiler_params=pltpu.CompilerParams(vmem_limit_bytes=48 * 2**20),
        cost_estimate=pl.CostEstimate(flops=flops, bytes_accessed=1, transcendentals=0),
    )(*args)


def block_dot(tile, first, same, other):
    total = 0.0
    for y in range(4):
        at = 128 * (first + y)
        total += dot(tile[:, at : at + 128], same[y, :, COLS])
        total += dot(tile[:, at + 512 : at + 640], other[y, :, COLS])
    return total


def near_body(tile, same, other, near):
    near[...] = block_dot(tile, 0, same, other)


def forward_body(tile, near, same, other, weight, cotangent, regroup, out, message):
    total = near[...] + block_dot(tile, 8, same, other)
    high = total.astype(BF16)
    low = (total - high.astype(F32)).astype(BF16)
    summed = dot(high, weight[...]) + dot(low, weight[...])
    sigmoid = jax.nn.sigmoid(summed)
    out[...] = summed * sigmoid
    slope = cotangent[...].astype(F32) * sigmoid * (1.0 + summed * (1.0 - sigmoid))
    slope = slope.astype(BF16)
    factor = dot(high, regroup[...]).astype(BF16)
    for y in range(4):
        message[y, :, COLS] = slope
        message[y, :, 1024:1280] = factor[:, 256 * y : 256 * y + 256]


def far_body(core, mirror, same, other, far):
    mine = core[0]
    total = 0.0
    for y in range(4):
        total += dot(mirror[2 * y + mine], same[y, :, COLS])
        total += dot(mirror[2 * y + 1 - mine], other[y, :, COLS])
    far[...] = total.astype(BF16)


def partial_body(same, other, partial):
    total = 0.0
    for y in range(4):
        total += dot(same[y, :, 1024:1152], same[y, :, COLS], 0, 0)
        total += dot(other[y, :, 1152:1280], other[y, :, COLS], 0, 0)
    partial[...] = total


def sum_x_body(pieces, out):
    total = pieces[0] + pieces[1] + pieces[2] + pieces[3]
    for z in range(8):
        rows = total[4 * z : 4 * z + 4].astype(BF16)
        out[z] = rows
        out[z + 8] = rows


def sum_z_body(pieces, out):
    total = pieces[0].astype(F32)
    for z in range(1, 16):
        total += pieces[z].astype(F32)
    for group in range(8):
        out[group] = total * (65536 ** -0.5)


def backward_body(tile, same, other, far, back_grad):
    total = block_dot(tile, 0, same, other) + far[...].astype(F32)
    back_grad[...] = total.astype(BF16)


def input_body(back_grad, weight, input_grad):
    input_grad[...] = dot(back_grad[...], weight[...], 1, 1)


def along_z(rows, step):
    pairs = []
    for z in range(16):
        for core in range(2):
            to = (z + (step if core == 0 else -step)) % 16
            pairs.append((z // 8 * 16 + core * 8 + z % 8, to // 8 * 16 + core * 8 + to % 8))
    return lax.ppermute(rows, ("zh", "co", "zl"), pairs)


def after(value, *others):
    return lax.optimization_barrier((value,) + others)[0]


def over_y(rows):
    return lax.all_to_all(jnp.broadcast_to(rows[None], (4,) + rows.shape), "y", 0, 0)


def other_core(rows):
    return lax.ppermute(rows, "co", SWAP)


def local(features, weight, cotangent, block_values, block_codes, block_count):
    zh, core = lax.axis_index("zh"), lax.axis_index("co")
    hidden = features.shape[1]
    grid_row = block_codes[0] % 512 // 32
    place = (grid_row // 8 ^ zh) * 8 + (grid_row % 2 ^ core) * 4 + grid_row % 8 // 2
    active = jnp.arange(16) < block_count[0]
    other = (grid_row[:, None] == jnp.arange(8)[None, :] + 8 * (1 - zh)) & active[:, None]
    mirror = jnp.einsum("km,kij->mji", other.astype(BF16), block_values[0], preferred_element_type=F32)
    mirror = mirror.astype(BF16)
    select = (place[:, None] == jnp.arange(16)[None, :]) & active[:, None]
    tile = jnp.einsum("km,kij->imj", select.astype(BF16), block_values[0], preferred_element_type=F32)
    tile = tile.astype(BF16).reshape(128, 2048)
    at = jnp.arange(hidden)
    group = 2 * (at // 256) + (at // 128 % 2 ^ core)
    source = 32 * (at // 4 % 32) + 4 * group + at % 4
    regroup = (jnp.arange(hidden)[:, None] == source[None, :]).astype(BF16)

    def shape(*dims, dtype=F32):
        return jax.ShapeDtypeStruct(dims, dtype)

    rows_f32, rows_bf16 = shape(128, hidden), shape(128, hidden, dtype=BF16)

    far = along_z(along_z(features, 1), 7)
    near_same = over_y(features)
    near_other = other_core(near_same)
    mirror = lax.all_to_all(after(mirror, near_same), ("y", "co"), 0, 0)
    near = call(near_body, rows_f32, tile, near_same, near_other)
    far_same = over_y(after(far, mirror))
    far_other = other_core(far_same)
    output, message = call(
        forward_body, (rows_f32, shape(4, 128, hidden + 256, dtype=BF16)),
        tile, near, far_same, far_other, weight, cotangent, regroup,
    )

    near_same = lax.all_to_all(message, "y", 0, 0)
    near_other = other_core(near_same)
    far = call(far_body, rows_bf16, core.reshape(1), mirror, near_same, near_other)
    far = along_z(far, 1)
    partial = call(partial_body, rows_f32, near_same, near_other)
    part = lax.all_to_all(partial.reshape(4, 32, hidden), "x", 0, 0)
    part = call(sum_x_body, shape(16, 4, hidden, dtype=BF16), part)
    part, far = lax.optimization_barrier((part, far))
    far = along_z(far, 7)
    part = lax.all_to_all(part, ("zh", "zl"), 0, 0)
    back_grad = call(
        backward_body, rows_bf16, tile, near_same, near_other, far, flops=10**11
    )
    part = call(sum_z_body, shape(8, 4, hidden), after(part, back_grad))
    part = lax.all_to_all(part, ("y", "co"), 0, 0)
    weight_grad = part.reshape(32, hidden)
    input_grad = call(input_body, rows_f32, back_grad, weight)
    return output, input_grad, weight_grad


def solution(mesh):
    fine = Mesh(mesh.devices.reshape(SIZES), AXES)
    rows = P(AXES)
    return jax.shard_map(
        local,
        mesh=fine,
        in_specs=(rows, P(), rows, rows, rows, rows),
        out_specs=(rows, rows, P(("x", "zl"))),
        check_vma=False,
    )
```

```python
import jax
import jax.numpy as jnp
from jax import lax
from jax.experimental import pallas as pl
from jax.experimental.pallas import tpu as pltpu
from jax.sharding import Mesh, PartitionSpec as P

AXES = ("zh", "y", "co", "x", "zl")
SIZES = (2, 4, 2, 4, 8)
BF16, F32 = jnp.bfloat16, jnp.float32
SWAP = [(0, 1), (1, 0)]
VMEM = pl.BlockSpec(memory_space=pltpu.VMEM)
SMEM = pl.BlockSpec(memory_space=pltpu.SMEM)
COLS = slice(0, 1024)


def dot(a, b, over_a=1, over_b=0):
    return lax.dot_general(a, b, (((over_a,), (over_b,)), ((), ())), preferred_element_type=F32)


def call(body, outs, *args, flops=1):
    return pl.pallas_call(
        body,
        out_shape=outs,
        in_specs=[SMEM if a.dtype == jnp.int32 else VMEM for a in args],
        out_specs=jax.tree.map(lambda _: VMEM, outs),
        compiler_params=pltpu.CompilerParams(vmem_limit_bytes=16 * 2**20),
        cost_estimate=pl.CostEstimate(flops=flops, bytes_accessed=1, transcendentals=0),
    )(*args)


def block_dot(tile, same, other):
    total = 0.0
    for y in range(4):
        at = 128 * y
        total += dot(tile[:, at : at + 128], same[y, :, COLS])
        total += dot(tile[:, at + 512 : at + 640], other[y, :, COLS])
    return total


def near_body(tile, same, other, near):
    near[...] = block_dot(tile, same, other)


def forward_body(near, far, weight, cotangent, regroup, out, message):
    total = near[...] + far[...].astype(F32)
    high = total.astype(BF16)
    low = (total - high.astype(F32)).astype(BF16)
    summed = dot(high, weight[...]) + dot(low, weight[...])
    sigmoid = jax.nn.sigmoid(summed)
    out[...] = summed * sigmoid
    slope = cotangent[...].astype(F32) * sigmoid * (1.0 + summed * (1.0 - sigmoid))
    slope = slope.astype(BF16)
    factor = dot(high, regroup[...]).astype(BF16)
    for y in range(4):
        message[y, :, COLS] = slope
        message[y, :, 1024:1280] = factor[:, 256 * y : 256 * y + 256]


def prepare_body(place, codes, count, values, features, message, tile):
    tile[...] = jnp.zeros(tile.shape, BF16)
    for y in range(4):
        message[y, :, COLS] = features[...]
        message[y, :, 1024:1280] = jnp.zeros((128, 256), BF16)

    def slot(k, carry):
        grid_row = lax.div(lax.rem(codes[0, k], 512), 32)
        y, other = lax.div(lax.rem(grid_row, 8), 2), lax.rem(grid_row + place[1], 2)
        own = lax.div(grid_row, 8) == place[0]

        @pl.when(own)
        def _():
            tile[:, pl.ds(pl.multiple_of(512 * other + 128 * y, 128), 128)] = values[0, k]

        @pl.when(jnp.logical_not(own))
        def _():
            message[y, :, pl.ds(pl.multiple_of(1024 + 128 * other, 128), 128)] = values[0, k]

        return carry

    lax.fori_loop(0, count[0], slot, 0)


def grouped(same, other):
    total = 0.0
    for y in range(4):
        total += dot(same[y, :, 1024:1152], same[y, :, COLS], 0, 0)
        total += dot(other[y, :, 1152:1280], other[y, :, COLS], 0, 0)
    return total


def first_far_body(same, other, far, mirror):
    far[...] = grouped(same, other).astype(BF16)
    for y in range(4):
        mirror[y] = same[y, :, 1024:1152]
        mirror[y + 4] = other[y, :, 1152:1280]


def far_body(mirror, same, other, far):
    total = 0.0
    for y in range(4):
        total += dot(mirror[y], same[y, :, COLS], 0, 0)
        total += dot(mirror[y + 4], other[y, :, COLS], 0, 0)
    far[...] = total.astype(BF16)


def partial_body(same, other, partial):
    partial[...] = grouped(same, other)


def sum_x_body(pieces, out):
    total = pieces[0] + pieces[1] + pieces[2] + pieces[3]
    for z in range(8):
        rows = total[4 * z : 4 * z + 4].astype(BF16)
        out[z] = rows
        out[z + 8] = rows


def sum_z_body(pieces, out):
    total = pieces[0].astype(F32)
    for z in range(1, 16):
        total += pieces[z].astype(F32)
    for group in range(8):
        out[group] = total * (65536 ** -0.5)


def backward_body(tile, same, other, far, weight, input_grad):
    total = block_dot(tile, same, other) + far[...].astype(F32)
    input_grad[...] = dot(total.astype(BF16), weight[...], 1, 1)


def partner(rows):
    return lax.ppermute(rows, "zh", SWAP)


def after(value, *others):
    return lax.optimization_barrier((value,) + others)[0]


def over_y(message):
    return lax.all_to_all(message, "y", 0, 0)


def other_core(rows):
    return lax.ppermute(rows, "co", SWAP)


def local(features, weight, cotangent, block_values, block_codes, block_count):
    zh, core = lax.axis_index("zh"), lax.axis_index("co")
    hidden = features.shape[1]
    at = jnp.arange(hidden)
    group = 2 * (at // 256) + (at // 128 % 2 ^ core)
    source = 32 * (at // 4 % 32) + 4 * group + at % 4
    regroup = (jnp.arange(hidden)[:, None] == source[None, :]).astype(BF16)

    def shape(*dims, dtype=F32):
        return jax.ShapeDtypeStruct(dims, dtype)

    rows_f32, rows_bf16 = shape(128, hidden), shape(128, hidden, dtype=BF16)
    message_shape = shape(4, 128, hidden + 256, dtype=BF16)

    message, tile = call(
        prepare_body, (message_shape, shape(128, 1024, dtype=BF16)),
        jnp.stack([zh, core]), block_codes, block_count, block_values, features,
    )
    same = over_y(message)
    other = other_core(same)
    far, mirror = call(first_far_body, (rows_bf16, shape(8, 128, 128, dtype=BF16)), same, other)
    far = partner(far)
    near = call(near_body, rows_f32, tile, same, other)
    output, message = call(
        forward_body, (rows_f32, message_shape), near, far, weight, cotangent, regroup
    )

    same = over_y(message)
    other = other_core(same)
    partial = call(partial_body, rows_f32, same, other)
    part = lax.all_to_all(partial.reshape(4, 32, hidden), "x", 0, 0)
    far = partner(call(far_body, rows_bf16, mirror, same, other))
    part = call(sum_x_body, shape(16, 4, hidden, dtype=BF16), part)
    part = lax.all_to_all(part, ("zh", "zl"), 0, 0)
    input_grad = call(backward_body, rows_f32, tile, same, other, far, weight, flops=10**11)
    part = call(sum_z_body, shape(8, 4, hidden), after(part, input_grad))
    part = lax.all_to_all(part, ("y", "co"), 0, 0)
    weight_grad = part.reshape(32, hidden)
    return output, input_grad, weight_grad


def solution(mesh):
    fine = Mesh(mesh.devices.reshape(SIZES), AXES)
    rows = P(AXES)
    return jax.shard_map(
        local,
        mesh=fine,
        in_specs=(rows, P(), rows, rows, rows, rows),
        out_specs=(rows, rows, P(("x", "zl"))),
        check_vma=False,
    )
```

```python
import jax
import jax.numpy as jnp
from jax import lax
from jax.experimental import pallas as pl
from jax.experimental.pallas import tpu as pltpu
from jax.sharding import Mesh, PartitionSpec as P

AXES = ("zh", "y", "co", "x", "zl")
SIZES = (2, 4, 2, 4, 8)
BF16, F32 = jnp.bfloat16, jnp.float32
SWAP = [(0, 1), (1, 0)]
VMEM = pl.BlockSpec(memory_space=pltpu.VMEM)
SMEM = pl.BlockSpec(memory_space=pltpu.SMEM)
COLS, FIRST, LAST = slice(0, 1024), slice(0, 512), slice(512, 1024)


def dot(a, b, over_a=1, over_b=0):
    return lax.dot_general(a, b, (((over_a,), (over_b,)), ((), ())), preferred_element_type=F32)


def call(body, outs, *args, flops=1):
    return pl.pallas_call(
        body,
        out_shape=outs,
        in_specs=[SMEM if a.dtype == jnp.int32 else VMEM for a in args],
        out_specs=jax.tree.map(lambda _: VMEM, outs),
        compiler_params=pltpu.CompilerParams(vmem_limit_bytes=16 * 2**20),
        cost_estimate=pl.CostEstimate(flops=flops, bytes_accessed=1, transcendentals=0),
    )(*args)


def prepare_body(place, codes, count, values, features, message, first, tile):
    tile[...] = jnp.zeros(tile.shape, BF16)
    first[...] = features[:, FIRST]
    for y in range(4):
        message[y, :, COLS] = features[...]
        message[y, :, 1024:1280] = jnp.zeros((128, 256), BF16)

    def slot(k, carry):
        grid_row = lax.div(lax.rem(codes[0, k], 512), 32)
        y, other = lax.div(lax.rem(grid_row, 8), 2), lax.rem(grid_row + place[1], 2)
        own = lax.div(grid_row, 8) == place[0]
        at = 512 * other + 128 * y + jnp.where(own, 0, 1024)
        tile[:, pl.ds(pl.multiple_of(at, 128), 128)] = values[0, k]

        @pl.when(jnp.logical_not(own))
        def _():
            message[y, :, pl.ds(pl.multiple_of(1024 + 128 * other, 128), 128)] = values[0, k]

        return carry

    lax.fori_loop(0, count[0], slot, 0)


def near_body(tile, same, other, near):
    total = 0.0
    for y in range(4):
        at = 128 * y
        total += dot(tile[:, at : at + 128], same[y, :, COLS])
        total += dot(tile[:, at + 512 : at + 640], other[y, :, COLS])
    near[...] = total


def whole(near, tile, last, same, other):
    first = near[:, FIRST]
    for y in range(4):
        at = 1024 + 128 * y
        first += dot(tile[:, at : at + 128], same[y])
        first += dot(tile[:, at + 512 : at + 640], other[y])
    return jnp.concatenate([first, near[:, LAST] + last[...].astype(F32)], axis=1)


def far_body(mirror, same, other, far):
    total = 0.0
    for y in range(4):
        total += dot(mirror[y], same[y, :, LAST], 0, 0)
        total += dot(mirror[y + 4], other[y, :, LAST], 0, 0)
    far[...] = total.astype(BF16)


def first_far_body(same, other, far, mirror):
    for y in range(4):
        mirror[y] = same[y, :, 1024:1152]
        mirror[y + 4] = other[y, :, 1152:1280]
    far_body(mirror, same, other, far)


def forward_body(near, tile, last, same, other, weight, cotangent, regroup, out, message, first):
    total = whole(near, tile, last, same, other)
    high = total.astype(BF16)
    low = (total - high.astype(F32)).astype(BF16)
    summed = dot(high, weight[...]) + dot(low, weight[...])
    sigmoid = jax.nn.sigmoid(summed)
    out[...] = summed * sigmoid
    slope = cotangent[...].astype(F32) * sigmoid * (1.0 + summed * (1.0 - sigmoid))
    slope = slope.astype(BF16)
    first[...] = slope[:, FIRST]
    factor = dot(high, regroup[...]).astype(BF16)
    for y in range(4):
        message[y, :, COLS] = slope
        message[y, :, 1024:1280] = factor[:, 256 * y : 256 * y + 256]


def backward_body(near, tile, last, same, other, weight, input_grad):
    total = whole(near, tile, last, same, other)
    input_grad[...] = dot(total.astype(BF16), weight[...], 1, 1)


def partial_body(same, other, partial):
    total = 0.0
    for y in range(4):
        total += dot(same[y, :, 1024:1152], same[y, :, COLS], 0, 0)
        total += dot(other[y, :, 1152:1280], other[y, :, COLS], 0, 0)
    partial[...] = total


def sum_x_body(pieces, out):
    total = pieces[0] + pieces[1] + pieces[2] + pieces[3]
    for z in range(8):
        rows = total[4 * z : 4 * z + 4].astype(BF16)
        out[z] = rows
        out[z + 8] = rows


def sum_z_body(pieces, out):
    total = pieces[0].astype(F32)
    for z in range(1, 16):
        total += pieces[z].astype(F32)
    for group in range(8):
        out[group] = total * (65536 ** -0.5)


def partner(rows):
    return lax.ppermute(rows, "zh", SWAP)


def over_y(message):
    return lax.all_to_all(message, "y", 0, 0)


def spread(rows):
    return over_y(jnp.broadcast_to(rows[None], (4,) + rows.shape))


def other_core(rows):
    return lax.ppermute(rows, "co", SWAP)


def after(value, *others):
    return lax.optimization_barrier((value,) + others)[0]


def local(features, weight, cotangent, block_values, block_codes, block_count):
    zh, core = lax.axis_index("zh"), lax.axis_index("co")
    hidden = features.shape[1]
    at = jnp.arange(hidden)
    group = 2 * (at // 256) + (at // 128 % 2 ^ core)
    source = 32 * (at // 4 % 32) + 4 * group + at % 4
    regroup = (jnp.arange(hidden)[:, None] == source[None, :]).astype(BF16)

    def shape(*dims, dtype=F32):
        return jax.ShapeDtypeStruct(dims, dtype)

    rows = shape(128, hidden)
    half = shape(128, hidden // 2, dtype=BF16)
    message_shape = shape(4, 128, hidden + 256, dtype=BF16)

    message, first, tile = call(
        prepare_body, (message_shape, half, shape(128, 2048, dtype=BF16)),
        jnp.stack([zh, core]), block_codes, block_count, block_values, features,
    )
    far = partner(first)
    same = over_y(message)
    other = other_core(after(same, far))
    far_same = spread(far)
    last, mirror = call(first_far_body, (half, shape(8, 128, 128, dtype=BF16)), same, other)
    last = partner(last)
    near = call(near_body, rows, tile, same, other)
    far_other = other_core(after(far_same, last))
    output, message, first = call(
        forward_body, (rows, message_shape, half),
        near, tile, last, far_same, far_other, weight, cotangent, regroup,
    )

    far = partner(first)
    same = over_y(message)
    other = other_core(after(same, far))
    far_same = spread(far)
    partial = call(partial_body, rows, same, other)
    far_other = other_core(after(far_same, partial))
    part = lax.all_to_all(partial.reshape(4, 32, hidden), "x", 0, 0)
    last = partner(call(far_body, half, mirror, same, other))
    near = call(near_body, rows, tile, same, other)
    part = call(sum_x_body, shape(16, 4, hidden, dtype=BF16), part)
    part = lax.all_to_all(after(part, far_same), ("zh", "zl"), 0, 0)
    input_grad = call(
        backward_body, rows, near, tile, last, far_same, far_other, weight, flops=10**11
    )
    part = call(sum_z_body, shape(8, 4, hidden), after(part, input_grad))
    part = lax.all_to_all(part, ("y", "co"), 0, 0)
    weight_grad = part.reshape(32, hidden)
    return output, input_grad, weight_grad


def solution(mesh):
    fine = Mesh(mesh.devices.reshape(SIZES), AXES)
    rows = P(AXES)
    return jax.shard_map(
        local,
        mesh=fine,
        in_specs=(rows, P(), rows, rows, rows, rows),
        out_specs=(rows, rows, P(("x", "zl"))),
        check_vma=False,
    )
```

```python
import jax
import jax.numpy as jnp
from jax import lax
from jax.experimental import pallas as pl
from jax.experimental.pallas import tpu as pltpu
from jax.sharding import Mesh, PartitionSpec as P

AXES = ("zh", "y", "co", "x", "zl")
SIZES = (2, 4, 2, 4, 8)
BF16, F32 = jnp.bfloat16, jnp.float32
SWAP = [(0, 1), (1, 0)]
VMEM = pl.BlockSpec(memory_space=pltpu.VMEM)
SMEM = pl.BlockSpec(memory_space=pltpu.SMEM)
COLS = slice(0, 1024)


def dot(a, b, over_a=1, over_b=0):
    return lax.dot_general(a, b, (((over_a,), (over_b,)), ((), ())), preferred_element_type=F32)


def call(body, outs, *args, flops=1):
    return pl.pallas_call(
        body,
        out_shape=outs,
        in_specs=[SMEM if a.dtype == jnp.int32 else VMEM for a in args],
        out_specs=jax.tree.map(lambda _: VMEM, outs),
        compiler_params=pltpu.CompilerParams(vmem_limit_bytes=16 * 2**20),
        cost_estimate=pl.CostEstimate(flops=flops, bytes_accessed=1, transcendentals=0),
    )(*args)


def second_body(tile, begun, same, other, near):
    near_body(tile, same, other, near)
    near[...] += begun[...]


def near_body(tile, same, other, near):
    total = 0.0
    for y in range(4):
        at = 128 * y
        total += dot(tile[:, at : at + 128], same[y, :, COLS])
        total += dot(tile[:, at + 512 : at + 640], other[y, :, COLS])
    near[...] = total


def forward_body(near, far, weight, cotangent, regroup, summed_out, message, own):
    total = near[...] + far[...].astype(F32)
    high = total.astype(BF16)
    low = (total - high.astype(F32)).astype(BF16)
    summed = dot(high, weight[...]) + dot(low, weight[...])
    sigmoid = jax.nn.sigmoid(summed)
    summed_out[...] = summed
    slope = cotangent[...].astype(F32) * sigmoid * (1.0 + summed * (1.0 - sigmoid))
    slope = slope.astype(BF16)
    own[...] = slope
    factor = dot(high, regroup[...]).astype(BF16)
    for y in range(4):
        message[y, :, COLS] = slope
        message[y, :, 1024:1280] = factor[:, 256 * y : 256 * y + 256]


def output_body(summed, out):
    out[...] = summed[...] * jax.nn.sigmoid(summed[...])


def start_body(tile, far, begun):
    begun[...] = dot(tile[:, 1024:1152], far[...])


def prepare_body(place, codes, count, values, features, message, tile):
    tile[...] = jnp.zeros(tile.shape, BF16)
    for y in range(4):
        message[y, :, COLS] = features[...]
        message[y, :, 1024:1280] = jnp.zeros((128, 256), BF16)

    def slot(k, carry):
        grid_row = lax.div(lax.rem(codes[0, k], 512), 32)
        y, other = lax.div(lax.rem(grid_row, 8), 2), lax.rem(grid_row + place[1], 2)
        own = lax.div(grid_row, 8) == place[0]

        at = 512 * other + jnp.where(own, 128 * y, 1024 + 128 * lax.rem(place[2] - y + 4, 4))
        tile[:, pl.ds(pl.multiple_of(at, 128), 128)] = values[0, k]

        @pl.when(jnp.logical_not(own))
        def _():
            message[y, :, pl.ds(pl.multiple_of(1024 + 128 * other, 128), 128)] = values[0, k]

        return carry

    lax.fori_loop(0, count[0], slot, 0)


def far_body(same, other, far):
    total = 0.0
    for y in range(4):
        total += dot(same[y, :, 1024:1152], same[y, :, COLS], 0, 0)
        total += dot(other[y, :, 1152:1280], other[y, :, COLS], 0, 0)
    far[...] = total.astype(BF16)


def partial_body(same, partial):
    total = 0.0
    for y in range(4):
        total += dot(same[y, :, 1024:1280], same[y, :, COLS], 0, 0)
    partial[...] = total


def sum_x_body(pieces, keep, send):
    total = pieces[0] + pieces[1] + pieces[2] + pieces[3]
    keep[...] = total[0:32]
    send[...] = total[32:64]


def sum_core_body(keep, received, out):
    total = keep[...] + received[...]
    for z in range(8):
        rows = total[4 * z : 4 * z + 4].astype(BF16)
        out[z] = rows
        out[z + 8] = rows


def sum_z_body(pieces, out):
    total = pieces[0].astype(F32)
    for z in range(1, 16):
        total += pieces[z].astype(F32)
    for group in range(8):
        out[group] = total * (65536 ** -0.5)


def backward_body(tile, near, weight, *refs):
    *rows, input_grad = refs
    total = near[...]
    for i, piece in enumerate(rows):
        total += dot(tile[:, 1152 + 128 * i : 1280 + 128 * i], piece[...])
    input_grad[...] = dot(total.astype(BF16), weight[...], 1, 1)


def partner(rows):
    return lax.ppermute(rows, "zh", SWAP)


def after(value, *others):
    return lax.optimization_barrier((value,) + others)[0]


def over_y(message):
    return lax.all_to_all(message, "y", 0, 0)


def other_core(rows):
    return lax.ppermute(rows, "co", SWAP)


def local(features, weight, cotangent, block_values, block_codes, block_count):
    zh, core = lax.axis_index("zh"), lax.axis_index("co")
    hidden = features.shape[1]
    at = jnp.arange(hidden)
    row = 8 * (at // 256) + 4 * (at // 32 % 2 ^ core) + at % 4
    source = 32 * (8 * (at // 64 % 4) + at // 4 % 8) + row
    regroup = (jnp.arange(hidden)[:, None] == source[None, :]).astype(BF16)

    def shape(*dims, dtype=F32):
        return jax.ShapeDtypeStruct(dims, dtype)

    rows_f32, rows_bf16 = shape(128, hidden), shape(128, hidden, dtype=BF16)
    message_shape = shape(4, 128, hidden + 256, dtype=BF16)

    message, tile = call(
        prepare_body, (message_shape, shape(128, 2048, dtype=BF16)),
        jnp.stack([zh, core, lax.axis_index("y")]), block_codes, block_count, block_values, features,
    )
    same = over_y(message)
    other = other_core(same)
    far = partner(call(far_body, rows_bf16, same, other))
    near = call(near_body, rows_f32, tile, same, other)
    summed, message, slope = call(
        forward_body, (rows_f32, message_shape, rows_bf16),
        near, far, weight, cotangent, regroup,
    )

    far = partner(slope)
    same = over_y(message)
    output = call(output_body, rows_f32, summed, flops=10**11)
    partial = call(partial_body, shape(256, hidden), after(same, output))
    part = lax.all_to_all(partial.reshape(4, 64, hidden), "x", 0, 0)
    begun = call(start_body, rows_f32, tile, far, flops=10**11)
    keep, send = call(
        sum_x_body, (shape(32, hidden), shape(32, hidden)), after(part, begun)
    )
    others = [lax.ppermute(far, "y", [(i, (i + k) % 4) for i in range(4)]) for k in (1, 2, 3)]
    other = other_core(after(same, keep))
    near = call(second_body, rows_f32, tile, begun, same, other)
    part = call(sum_core_body, shape(16, 4, hidden, dtype=BF16), keep, other_core(send))
    part = lax.all_to_all(part, ("zh", "zl"), 0, 0)
    swapped = [other_core(v) for v in (far, *others)]
    input_grad = call(backward_body, rows_f32, tile, near, weight, *others, *swapped)
    part = call(sum_z_body, shape(8, 4, hidden), after(part, input_grad))
    part = lax.all_to_all(part, ("y", "co"), 0, 0)
    weight_grad = part.reshape(32, hidden)
    return output, input_grad, weight_grad


def solution(mesh):
    fine = Mesh(mesh.devices.reshape(SIZES), AXES)
    rows = P(AXES)
    return jax.shard_map(
        local,
        mesh=fine,
        in_specs=(rows, P(), rows, rows, rows, rows),
        out_specs=(rows, rows, P(("x", "zl"))),
        check_vma=False,
    )
```

```python
import jax
import jax.numpy as jnp
from jax import lax
from jax.experimental import pallas as pl
from jax.experimental.pallas import tpu as pltpu
from jax.sharding import Mesh, PartitionSpec as P

AXES = ("zh", "y", "co", "x", "zl")
SIZES = (2, 4, 2, 4, 8)
BF16, F32 = jnp.bfloat16, jnp.float32
SWAP = [(0, 1), (1, 0)]
VMEM = pl.BlockSpec(memory_space=pltpu.VMEM)
SMEM = pl.BlockSpec(memory_space=pltpu.SMEM)
COLS = slice(0, 1024)


def dot(a, b, over_a=1, over_b=0):
    return lax.dot_general(a, b, (((over_a,), (over_b,)), ((), ())), preferred_element_type=F32)


def call(body, outs, *args, flops=1):
    return pl.pallas_call(
        body,
        out_shape=outs,
        in_specs=[SMEM if a.dtype == jnp.int32 else VMEM for a in args],
        out_specs=jax.tree.map(lambda _: VMEM, outs),
        compiler_params=pltpu.CompilerParams(vmem_limit_bytes=16 * 2**20),
        cost_estimate=pl.CostEstimate(flops=flops, bytes_accessed=1, transcendentals=0),
    )(*args)


def second_body(tile, begun, same, other, near):
    near_body(tile, same, other, near)
    near[...] += begun[...]


def near_body(tile, same, other, near):
    total = 0.0
    for y in range(4):
        at = 128 * y
        total += dot(tile[:, at : at + 128], same[y, :, COLS])
        total += dot(tile[:, at + 512 : at + 640], other[y, :, COLS])
    near[...] = total


def forward_body(near, far, weight, cotangent, regroup, summed_out, message, own):
    total = near[...] + far[...].astype(F32)
    high = total.astype(BF16)
    low = (total - high.astype(F32)).astype(BF16)
    summed = dot(high, weight[...]) + dot(low, weight[...])
    sigmoid = jax.nn.sigmoid(summed)
    summed_out[...] = summed
    slope = cotangent[...].astype(F32) * sigmoid * (1.0 + summed * (1.0 - sigmoid))
    slope = slope.astype(BF16)
    own[...] = slope
    factor = dot(high, regroup[...]).astype(BF16)
    for y in range(4):
        message[y, :, COLS] = slope
        message[y, :, 1024:1280] = factor[:, 256 * y : 256 * y + 256]


def output_body(summed, out):
    out[...] = summed[...] * jax.nn.sigmoid(summed[...])


def start_body(tile, far, begun):
    begun[...] = dot(tile[:, 1024:1152], far[...])


def prepare_body(place, codes, count, values_hbm, features, message, tile, values, sems):
    copies = [pltpu.make_async_copy(values_hbm.at[0], values, sems.at[4])]
    for y in range(4):
        copies.append(pltpu.make_async_copy(features, message.at[y, :, COLS], sems.at[y]))
    for copy in copies:
        copy.start()
    tile[...] = jnp.zeros(tile.shape, BF16)
    for y in range(4):
        message[y, :, 1024:1280] = jnp.zeros((128, 256), BF16)
    copies[0].wait()

    def slot(k, carry):
        grid_row = lax.div(lax.rem(codes[0, k], 512), 32)
        y, other = lax.div(lax.rem(grid_row, 8), 2), lax.rem(grid_row + place[1], 2)
        own = lax.div(grid_row, 8) == place[0]

        at = 512 * other + jnp.where(own, 128 * y, 1024 + 128 * lax.rem(place[2] - y + 4, 4))
        tile[:, pl.ds(pl.multiple_of(at, 128), 128)] = values[k]

        @pl.when(jnp.logical_not(own))
        def _():
            message[y, :, pl.ds(pl.multiple_of(1024 + 128 * other, 128), 128)] = values[k]

        return carry

    lax.fori_loop(0, count[0], slot, 0)
    for copy in copies[1:]:
        copy.wait()


def far_body(same, other, far):
    total = 0.0
    for y in range(4):
        total += dot(same[y, :, 1024:1152], same[y, :, COLS], 0, 0)
        total += dot(other[y, :, 1152:1280], other[y, :, COLS], 0, 0)
    far[...] = total.astype(BF16)


def partial_body(same, other, partial):
    total = 0.0
    for y in range(4):
        total += dot(same[y, :, 1024:1152], same[y, :, COLS], 0, 0)
        total += dot(other[y, :, 1152:1280], other[y, :, COLS], 0, 0)
    partial[...] = total


def sum_x_body(pieces, out):
    total = pieces[0] + pieces[1] + pieces[2] + pieces[3]
    for z in range(8):
        rows = total[4 * z : 4 * z + 4].astype(BF16)
        out[z] = rows
        out[z + 8] = rows


def sum_z_body(pieces, out):
    total = pieces[0].astype(F32)
    for z in range(1, 16):
        total += pieces[z].astype(F32)
    for group in range(8):
        out[group] = total * (65536 ** -0.5)


def backward_body(tile, near, weight, *refs):
    *rows, input_grad = refs
    total = near[...]
    for i, piece in enumerate(rows):
        total += dot(tile[:, 1152 + 128 * i : 1280 + 128 * i], piece[...])
    input_grad[...] = dot(total.astype(BF16), weight[...], 1, 1)


def partner(rows):
    return lax.ppermute(rows, "zh", SWAP)


def after(value, *others):
    return lax.optimization_barrier((value,) + others)[0]


def over_y(message):
    return lax.all_to_all(message, "y", 0, 0)


def other_core(rows):
    return lax.ppermute(rows, "co", SWAP)


def local(features, weight, cotangent, block_values, block_codes, block_count):
    zh, core = lax.axis_index("zh"), lax.axis_index("co")
    hidden = features.shape[1]
    at = jnp.arange(hidden)
    group = 2 * (at // 256) + (at // 128 % 2 ^ core)
    source = 32 * (at // 4 % 32) + 4 * group + at % 4
    regroup = (jnp.arange(hidden)[:, None] == source[None, :]).astype(BF16)

    def shape(*dims, dtype=F32):
        return jax.ShapeDtypeStruct(dims, dtype)

    rows_f32, rows_bf16 = shape(128, hidden), shape(128, hidden, dtype=BF16)
    message_shape = shape(4, 128, hidden + 256, dtype=BF16)

    message, tile = pl.pallas_call(
        prepare_body,
        out_shape=(message_shape, shape(128, 2048, dtype=BF16)),
        in_specs=[SMEM] * 3 + [pl.BlockSpec(memory_space=pl.ANY)] * 2,
        out_specs=(VMEM, VMEM),
        scratch_shapes=[
            pltpu.VMEM(block_values.shape[1:], BF16), pltpu.SemaphoreType.DMA((5,)),
        ],
        compiler_params=pltpu.CompilerParams(vmem_limit_bytes=16 * 2**20),
    )(
        jnp.stack([zh, core, lax.axis_index("y")]), block_codes, block_count, block_values, features,
    )
    same = over_y(message)
    other = other_core(same)
    far = partner(call(far_body, rows_bf16, same, other))
    near = call(near_body, rows_f32, tile, same, other)
    summed, message, slope = call(
        forward_body, (rows_f32, message_shape, rows_bf16),
        near, far, weight, cotangent, regroup,
    )

    far = partner(slope)
    same = over_y(message)
    output = call(output_body, rows_f32, summed, flops=10**11)
    other = other_core(after(same, output))
    begun = call(start_body, rows_f32, tile, far, flops=10**11)
    partial = call(partial_body, rows_f32, same, after(other, begun))
    part = lax.all_to_all(partial.reshape(4, 32, hidden), "x", 0, 0)
    others = [lax.ppermute(far, "y", [(i, (i + k) % 4) for i in range(4)]) for k in (1, 2, 3)]
    near = call(second_body, rows_f32, tile, begun, same, other)
    part = call(sum_x_body, shape(16, 4, hidden, dtype=BF16), after(part, *others))
    part = lax.all_to_all(part, ("zh", "zl"), 0, 0)
    swapped = [other_core(v) for v in (far, *others)]
    input_grad = call(backward_body, rows_f32, tile, near, weight, *others, *swapped)
    part = call(sum_z_body, shape(8, 4, hidden), part)
    part = lax.all_to_all(part, ("y", "co"), 0, 0)
    weight_grad = part.reshape(32, hidden)
    return output, input_grad, weight_grad


def solution(mesh):
    fine = Mesh(mesh.devices.reshape(SIZES), AXES)
    rows = P(AXES)
    return jax.shard_map(
        local,
        mesh=fine,
        in_specs=(rows, P(), rows, rows, rows, rows),
        out_specs=(rows, rows, P(("x", "zl"))),
        check_vma=False,
    )
```

```python
import jax
import jax.numpy as jnp
from jax import lax
from jax.experimental import pallas as pl
from jax.experimental.pallas import tpu as pltpu
from jax.sharding import Mesh, PartitionSpec as P

AXES = ("zh", "y", "co", "x", "zl")
SIZES = (2, 4, 2, 4, 8)
BF16, F32 = jnp.bfloat16, jnp.float32
SWAP = [(0, 1), (1, 0)]
VMEM = pl.BlockSpec(memory_space=pltpu.VMEM)
SMEM = pl.BlockSpec(memory_space=pltpu.SMEM)
COLS = slice(0, 1024)


def dot(a, b, over_a=1, over_b=0):
    return lax.dot_general(a, b, (((over_a,), (over_b,)), ((), ())), preferred_element_type=F32)


def call(body, outs, *args, flops=1):
    return pl.pallas_call(
        body,
        out_shape=outs,
        in_specs=[SMEM if a.dtype == jnp.int32 else VMEM for a in args],
        out_specs=jax.tree.map(lambda _: VMEM, outs),
        compiler_params=pltpu.CompilerParams(vmem_limit_bytes=16 * 2**20),
        cost_estimate=pl.CostEstimate(flops=flops, bytes_accessed=1, transcendentals=0),
    )(*args)


def block_dot(tile, same, other):
    total = 0.0
    for y in range(4):
        at = 128 * y
        total += dot(tile[:, at : at + 128], same[y, :, COLS])
        total += dot(tile[:, at + 512 : at + 640], other[y, :, COLS])
    return total


def near_body(tile, same, other, near):
    near[...] = block_dot(tile, same, other)


def forward_body(near, far, weight, cotangent, regroup, out, message):
    total = near[...] + far[...].astype(F32)
    high = total.astype(BF16)
    low = (total - high.astype(F32)).astype(BF16)
    summed = dot(high, weight[...]) + dot(low, weight[...])
    sigmoid = jax.nn.sigmoid(summed)
    out[...] = summed * sigmoid
    slope = cotangent[...].astype(F32) * sigmoid * (1.0 + summed * (1.0 - sigmoid))
    slope = slope.astype(BF16)
    factor = dot(high, regroup[...]).astype(BF16)
    for y in range(4):
        message[y, :, COLS] = slope
        message[y, :, 1024:1280] = factor[:, 256 * y : 256 * y + 256]


def prepare_body(place, codes, count, values_hbm, features, message, tile, values, sems):
    copies = [pltpu.make_async_copy(values_hbm.at[0], values, sems.at[4])]
    for y in range(4):
        copies.append(pltpu.make_async_copy(features, message.at[y, :, COLS], sems.at[y]))
    for copy in copies:
        copy.start()
    tile[...] = jnp.zeros(tile.shape, BF16)
    for y in range(4):
        message[y, :, 1024:1280] = jnp.zeros((128, 256), BF16)
    copies[0].wait()

    def slot(k, carry):
        grid_row = lax.div(lax.rem(codes[0, k], 512), 32)
        y, other = lax.div(lax.rem(grid_row, 8), 2), lax.rem(grid_row + place[1], 2)
        own = lax.div(grid_row, 8) == place[0]

        @pl.when(own)
        def _():
            tile[:, pl.ds(pl.multiple_of(512 * other + 128 * y, 128), 128)] = values[k]

        @pl.when(jnp.logical_not(own))
        def _():
            message[y, :, pl.ds(pl.multiple_of(1024 + 128 * other, 128), 128)] = values[k]

        return carry

    lax.fori_loop(0, count[0], slot, 0)
    for copy in copies[1:]:
        copy.wait()


def grouped(same, other):
    total = 0.0
    for y in range(4):
        total += dot(same[y, :, 1024:1152], same[y, :, COLS], 0, 0)
        total += dot(other[y, :, 1152:1280], other[y, :, COLS], 0, 0)
    return total


def first_far_body(same, other, far, mirror):
    far[...] = grouped(same, other).astype(BF16)
    for y in range(4):
        mirror[y] = same[y, :, 1024:1152]
        mirror[y + 4] = other[y, :, 1152:1280]


def far_body(mirror, same, other, far):
    total = 0.0
    for y in range(4):
        total += dot(mirror[y], same[y, :, COLS], 0, 0)
        total += dot(mirror[y + 4], other[y, :, COLS], 0, 0)
    far[...] = total.astype(BF16)


def partial_body(same, other, partial):
    partial[...] = grouped(same, other)


def sum_x_body(pieces, out):
    total = pieces[0] + pieces[1] + pieces[2] + pieces[3]
    for z in range(8):
        rows = total[4 * z : 4 * z + 4].astype(BF16)
        out[z] = rows
        out[z + 8] = rows


def sum_z_body(pieces, out):
    total = pieces[0].astype(F32)
    for z in range(1, 16):
        total += pieces[z].astype(F32)
    for group in range(8):
        out[group] = total * (65536 ** -0.5)


def backward_body(tile, same, other, far, weight, input_grad):
    total = block_dot(tile, same, other) + far[...].astype(F32)
    input_grad[...] = dot(total.astype(BF16), weight[...], 1, 1)


def partner(rows):
    return lax.ppermute(rows, "zh", SWAP)


def after(value, *others):
    return lax.optimization_barrier((value,) + others)[0]


def over_y(message):
    return lax.all_to_all(message, "y", 0, 0)


def other_core(rows):
    return lax.ppermute(rows, "co", SWAP)


def local(features, weight, cotangent, block_values, block_codes, block_count):
    zh, core = lax.axis_index("zh"), lax.axis_index("co")
    hidden = features.shape[1]
    at = jnp.arange(hidden)
    group = 2 * (at // 256) + (at // 128 % 2 ^ core)
    source = 32 * (at // 4 % 32) + 4 * group + at % 4
    regroup = (jnp.arange(hidden)[:, None] == source[None, :]).astype(BF16)

    def shape(*dims, dtype=F32):
        return jax.ShapeDtypeStruct(dims, dtype)

    rows_f32, rows_bf16 = shape(128, hidden), shape(128, hidden, dtype=BF16)
    message_shape = shape(4, 128, hidden + 256, dtype=BF16)

    message, tile = pl.pallas_call(
        prepare_body,
        out_shape=(message_shape, shape(128, 1024, dtype=BF16)),
        in_specs=[SMEM] * 3 + [pl.BlockSpec(memory_space=pltpu.MemorySpace.HBM)] * 2,
        out_specs=(VMEM, VMEM),
        scratch_shapes=[
            pltpu.VMEM(block_values.shape[1:], BF16), pltpu.SemaphoreType.DMA((5,)),
        ],
        compiler_params=pltpu.CompilerParams(vmem_limit_bytes=16 * 2**20),
    )(
        jnp.stack([zh, core]), block_codes, block_count,
        pltpu.with_memory_space_constraint(block_values, pltpu.MemorySpace.HBM),
        pltpu.with_memory_space_constraint(features, pltpu.MemorySpace.HBM),
    )
    same = over_y(message)
    other = other_core(same)
    far, mirror = call(first_far_body, (rows_bf16, shape(8, 128, 128, dtype=BF16)), same, other)
    far = partner(far)
    near = call(near_body, rows_f32, tile, same, other)
    output, message = call(
        forward_body, (rows_f32, message_shape), near, far, weight, cotangent, regroup
    )

    same = over_y(message)
    other = other_core(same)
    partial = call(partial_body, rows_f32, same, other)
    part = lax.all_to_all(partial.reshape(4, 32, hidden), "x", 0, 0)
    far = call(far_body, rows_bf16, mirror, same, other)
    part = call(sum_x_body, shape(16, 4, hidden, dtype=BF16), after(part, far))
    part = lax.all_to_all(part, ("zh", "zl"), 0, 0)
    far = partner(far)
    input_grad = call(backward_body, rows_f32, tile, same, other, far, weight)
    part = call(sum_z_body, shape(8, 4, hidden), part)
    part = lax.all_to_all(part, ("y", "co"), 0, 0)
    weight_grad = part.reshape(32, hidden)
    return output, input_grad, weight_grad


def solution(mesh):
    fine = Mesh(mesh.devices.reshape(SIZES), AXES)
    rows = P(AXES)
    return jax.shard_map(
        local,
        mesh=fine,
        in_specs=(rows, P(), rows, rows, rows, rows),
        out_specs=(rows, rows, P(("x", "zl"))),
        check_vma=False,
    )
```

```python
import jax
import jax.numpy as jnp
from jax import lax
from jax.experimental import pallas as pl
from jax.experimental.pallas import tpu as pltpu
from jax.sharding import Mesh, PartitionSpec as P

AXES = ("zh", "y", "co", "x", "zl")
SIZES = (2, 4, 2, 4, 8)
BF16, F32 = jnp.bfloat16, jnp.float32
SWAP = [(0, 1), (1, 0)]
VMEM = pl.BlockSpec(memory_space=pltpu.VMEM)
HBM = pl.BlockSpec(memory_space=pltpu.MemorySpace.HBM)
SMEM = pl.BlockSpec(memory_space=pltpu.SMEM)
COLS = slice(0, 1024)


def dot(a, b, over_a=1, over_b=0):
    return lax.dot_general(a, b, (((over_a,), (over_b,)), ((), ())), preferred_element_type=F32)


def call(body, outs, *args, flops=1):
    return pl.pallas_call(
        body,
        out_shape=outs,
        in_specs=[SMEM if a.dtype == jnp.int32 else VMEM for a in args],
        out_specs=jax.tree.map(lambda _: VMEM, outs),
        compiler_params=pltpu.CompilerParams(vmem_limit_bytes=16 * 2**20),
        cost_estimate=pl.CostEstimate(flops=flops, bytes_accessed=1, transcendentals=0),
    )(*args)


def block_dot(tile, same, other):
    total = 0.0
    for y in range(4):
        at = 128 * y
        total += dot(tile[:, at : at + 128], same[y, :, COLS])
        total += dot(tile[:, at + 512 : at + 640], other[y, :, COLS])
    return total


def near_body(tile, same, other, near):
    near[...] = block_dot(tile, same, other)


def forward_body(near, far, weight, cotangent, regroup, out, message):
    total = near[...] + far[...].astype(F32)
    high = total.astype(BF16)
    low = (total - high.astype(F32)).astype(BF16)
    summed = dot(high, weight[...]) + dot(low, weight[...])
    sigmoid = jax.nn.sigmoid(summed)
    out[...] = summed * sigmoid
    slope = cotangent[...].astype(F32) * sigmoid * (1.0 + summed * (1.0 - sigmoid))
    slope = slope.astype(BF16)
    factor = dot(high, regroup[...]).astype(BF16)
    for y in range(4):
        message[y, :, COLS] = slope
        message[y, :, 1024:1280] = factor[:, 256 * y : 256 * y + 256]


def prepare_body(place, count, codes_hbm, values_hbm, features, message, tile, codes, values, sems):
    copies = [
        pltpu.make_async_copy(codes_hbm, codes, sems.at[5]),
        pltpu.make_async_copy(values_hbm.at[0], values, sems.at[4]),
    ]
    for y in range(4):
        copies.append(pltpu.make_async_copy(features, message.at[y, :, COLS], sems.at[y]))
    for copy in copies:
        copy.start()
    tile[...] = jnp.zeros(tile.shape, BF16)
    for y in range(4):
        message[y, :, 1024:1280] = jnp.zeros((128, 256), BF16)
    copies[0].wait()
    copies[1].wait()

    def slot(k, carry):
        grid_row = lax.div(lax.rem(codes[0, k], 512), 32)
        y, other = lax.div(lax.rem(grid_row, 8), 2), lax.rem(grid_row + place[1], 2)
        own = lax.div(grid_row, 8) == place[0]

        @pl.when(own)
        def _():
            tile[:, pl.ds(pl.multiple_of(512 * other + 128 * y, 128), 128)] = values[k]

        @pl.when(jnp.logical_not(own))
        def _():
            message[y, :, pl.ds(pl.multiple_of(1024 + 128 * other, 128), 128)] = values[k]

        return carry

    lax.fori_loop(0, count[0], slot, 0)
    for copy in copies[2:]:
        copy.wait()


def grouped(same, other):
    total = 0.0
    for y in range(4):
        total += dot(same[y, :, 1024:1152], same[y, :, COLS], 0, 0)
        total += dot(other[y, :, 1152:1280], other[y, :, COLS], 0, 0)
    return total


def first_far_body(same, other, far, mirror):
    far[...] = grouped(same, other).astype(BF16)
    for y in range(4):
        mirror[y] = same[y, :, 1024:1152]
        mirror[y + 4] = other[y, :, 1152:1280]


def sums_body(mirror, same, other, far_hbm, partial_hbm, far, partial, sems):
    far_here = 0.0
    for y in range(4):
        far_here += dot(mirror[y], same[y, :, COLS], 0, 0)
        far_here += dot(mirror[y + 4], other[y, :, COLS], 0, 0)
    far[...] = far_here.astype(BF16)
    far_copy = pltpu.make_async_copy(far, far_hbm, sems.at[0])
    far_copy.start()
    partial[...] = grouped(same, other)
    partial_copy = pltpu.make_async_copy(partial, partial_hbm, sems.at[1])
    partial_copy.start()
    far_copy.wait()
    partial_copy.wait()


def sum_x_body(pieces, out):
    total = pieces[0] + pieces[1] + pieces[2] + pieces[3]
    for z in range(8):
        rows = total[4 * z : 4 * z + 4].astype(BF16)
        out[z] = rows
        out[z + 8] = rows


def sum_z_body(pieces, out):
    total = pieces[0].astype(F32)
    for z in range(1, 16):
        total += pieces[z].astype(F32)
    for group in range(8):
        out[group] = total * (65536 ** -0.5)


def backward_body(tile, same, other, far, weight, input_grad):
    total = block_dot(tile, same, other) + far[...].astype(F32)
    input_grad[...] = dot(total.astype(BF16), weight[...], 1, 1)


def partner(rows):
    return lax.ppermute(rows, "zh", SWAP)


def after(value, *others):
    return lax.optimization_barrier((value,) + others)[0]


def over_y(message):
    return lax.all_to_all(message, "y", 0, 0)


def other_core(rows):
    return lax.ppermute(rows, "co", SWAP)


def local(features, weight, cotangent, block_values, block_codes, block_count):
    zh, core = lax.axis_index("zh"), lax.axis_index("co")
    hidden = features.shape[1]
    at = jnp.arange(hidden)
    group = 2 * (at // 256) + (at // 128 % 2 ^ core)
    source = 32 * (at // 4 % 32) + 4 * group + at % 4
    regroup = (jnp.arange(hidden)[:, None] == source[None, :]).astype(BF16)

    def shape(*dims, dtype=F32):
        return jax.ShapeDtypeStruct(dims, dtype)

    rows_f32, rows_bf16 = shape(128, hidden), shape(128, hidden, dtype=BF16)
    message_shape = shape(4, 128, hidden + 256, dtype=BF16)

    message, tile = pl.pallas_call(
        prepare_body,
        out_shape=(message_shape, shape(128, 1024, dtype=BF16)),
        in_specs=[SMEM] * 2 + [HBM] * 3,
        out_specs=(VMEM, VMEM),
        scratch_shapes=[
            pltpu.SMEM(block_codes.shape, jnp.int32),
            pltpu.VMEM(block_values.shape[1:], BF16),
            pltpu.SemaphoreType.DMA((6,)),
        ],
        compiler_params=pltpu.CompilerParams(vmem_limit_bytes=16 * 2**20),
    )(
        jnp.stack([zh, core]), block_count,
        *(
            pltpu.with_memory_space_constraint(a, pltpu.MemorySpace.HBM)
            for a in (block_codes, block_values, features)
        ),
    )
    same = over_y(message)
    other = other_core(same)
    far, mirror = call(first_far_body, (rows_bf16, shape(8, 128, 128, dtype=BF16)), same, other)
    far = partner(far)
    near = call(near_body, rows_f32, tile, same, other)
    output, message = call(
        forward_body, (rows_f32, message_shape), near, far, weight, cotangent, regroup
    )

    same = over_y(message)
    other = other_core(same)
    far, partial = pl.pallas_call(
        sums_body,
        out_shape=(
            pltpu.HBM(rows_bf16.shape, BF16), pltpu.HBM(rows_f32.shape, F32),
        ),
        in_specs=[VMEM] * 3,
        out_specs=(HBM, HBM),
        scratch_shapes=[
            pltpu.VMEM(rows_bf16.shape, BF16),
            pltpu.VMEM(rows_f32.shape, F32),
            pltpu.SemaphoreType.DMA((2,)),
        ],
        compiler_params=pltpu.CompilerParams(vmem_limit_bytes=16 * 2**20),
        cost_estimate=pl.CostEstimate(flops=1, bytes_accessed=1, transcendentals=0),
    )(mirror, same, other)
    part = lax.all_to_all(partial.reshape(4, 32, hidden), "x", 0, 0)
    far = partner(far)
    part = call(sum_x_body, shape(16, 4, hidden, dtype=BF16), part)
    part = lax.all_to_all(part, ("zh", "zl"), 0, 0)
    input_grad = call(backward_body, rows_f32, tile, same, other, far, weight, flops=10**11)
    part = call(sum_z_body, shape(8, 4, hidden), after(part, input_grad))
    part = lax.all_to_all(part, ("y", "co"), 0, 0)
    weight_grad = part.reshape(32, hidden)
    return output, input_grad, weight_grad


def solution(mesh):
    fine = Mesh(mesh.devices.reshape(SIZES), AXES)
    rows = P(AXES)
    return jax.shard_map(
        local,
        mesh=fine,
        in_specs=(rows, P(), rows, rows, rows, rows),
        out_specs=(rows, rows, P(("x", "zl"))),
        check_vma=False,
    )
```

```python
import jax
import jax.numpy as jnp
from jax import lax
from jax.experimental import pallas as pl
from jax.experimental.pallas import tpu as pltpu
from jax.sharding import Mesh, PartitionSpec as P

AXES = ("zh", "y", "co", "x", "zl")
SIZES = (2, 4, 2, 4, 8)
BF16, F32 = jnp.bfloat16, jnp.float32
SWAP = [(0, 1), (1, 0)]
VMEM = pl.BlockSpec(memory_space=pltpu.VMEM)
HBM = pl.BlockSpec(memory_space=pltpu.MemorySpace.HBM)
SMEM = pl.BlockSpec(memory_space=pltpu.SMEM)
COLS = slice(0, 1024)


def dot(a, b, over_a=1, over_b=0):
    return lax.dot_general(a, b, (((over_a,), (over_b,)), ((), ())), preferred_element_type=F32)


def call(body, outs, *args, flops=1):
    return pl.pallas_call(
        body,
        out_shape=outs,
        in_specs=[SMEM if a.dtype == jnp.int32 else VMEM for a in args],
        out_specs=jax.tree.map(lambda _: VMEM, outs),
        compiler_params=pltpu.CompilerParams(vmem_limit_bytes=16 * 2**20),
        cost_estimate=pl.CostEstimate(flops=flops, bytes_accessed=1, transcendentals=0),
    )(*args)


def block_dot(tile, same, other):
    total = 0.0
    for y in range(4):
        at = 128 * y
        total += dot(tile[:, at : at + 128], same[y, :, COLS])
        total += dot(tile[:, at + 512 : at + 640], other[y, :, COLS])
    return total


def near_body(tile, same, other, near):
    near[...] = block_dot(tile, same, other)


def forward_body(near, far, weight, cotangent, regroup, out, message):
    total = near[...] + far[...].astype(F32)
    high = total.astype(BF16)
    low = (total - high.astype(F32)).astype(BF16)
    summed = dot(high, weight[...]) + dot(low, weight[...])
    sigmoid = jax.nn.sigmoid(summed)
    out[...] = summed * sigmoid
    slope = cotangent[...].astype(F32) * sigmoid * (1.0 + summed * (1.0 - sigmoid))
    slope = slope.astype(BF16)
    factor = dot(high, regroup[...]).astype(BF16)
    for y in range(4):
        message[y, :, COLS] = slope
        message[y, :, 1024:1280] = factor[:, 256 * y : 256 * y + 256]


def prepare_body(place, count, codes_hbm, values_hbm, features, message, tile, codes, values, sems):
    copies = [
        pltpu.make_async_copy(codes_hbm, codes, sems.at[5]),
        pltpu.make_async_copy(values_hbm.at[0], values, sems.at[4]),
    ]
    for y in range(4):
        copies.append(pltpu.make_async_copy(features, message.at[y, :, COLS], sems.at[y]))
    for copy in copies:
        copy.start()
    tile[...] = jnp.zeros(tile.shape, BF16)
    for y in range(4):
        message[y, :, 1024:1280] = jnp.zeros((128, 256), BF16)
    copies[0].wait()
    copies[1].wait()

    def slot(k, carry):
        grid_row = lax.div(lax.rem(codes[0, k], 512), 32)
        y, other = lax.div(lax.rem(grid_row, 8), 2), lax.rem(grid_row + place[1], 2)
        own = lax.div(grid_row, 8) == place[0]

        @pl.when(own)
        def _():
            tile[:, pl.ds(pl.multiple_of(512 * other + 128 * y, 128), 128)] = values[k]

        @pl.when(jnp.logical_not(own))
        def _():
            message[y, :, pl.ds(pl.multiple_of(1024 + 128 * other, 128), 128)] = values[k]

        return carry

    lax.fori_loop(0, count[0], slot, 0)
    for copy in copies[2:]:
        copy.wait()


def grouped(same, other):
    total = 0.0
    for y in range(4):
        total += dot(same[y, :, 1024:1152], same[y, :, COLS], 0, 0)
        total += dot(other[y, :, 1152:1280], other[y, :, COLS], 0, 0)
    return total


def first_far_body(same, other, far, mirror):
    far[...] = grouped(same, other).astype(BF16)
    for y in range(4):
        mirror[y] = same[y, :, 1024:1152]
        mirror[y + 4] = other[y, :, 1152:1280]


def sums_body(mirror, same, other, far_hbm, partial_hbm, far, partial, sems):
    far_here = 0.0
    for y in range(4):
        far_here += dot(mirror[y], same[y, :, COLS], 0, 0)
        far_here += dot(mirror[y + 4], other[y, :, COLS], 0, 0)
    far[...] = far_here.astype(BF16)
    far_copy = pltpu.make_async_copy(far, far_hbm, sems.at[0])
    far_copy.start()
    partial[...] = grouped(same, other).astype(BF16)
    partial_copy = pltpu.make_async_copy(partial, partial_hbm, sems.at[1])
    partial_copy.start()
    far_copy.wait()
    partial_copy.wait()


def sum_x_body(pieces, out):
    total = pieces[0].astype(F32) + pieces[1].astype(F32)
    total += pieces[2].astype(F32) + pieces[3].astype(F32)
    for z in range(8):
        rows = total[4 * z : 4 * z + 4].astype(BF16)
        out[z] = rows
        out[z + 8] = rows


def sum_z_body(pieces, out):
    total = pieces[0].astype(F32)
    for z in range(1, 16):
        total += pieces[z].astype(F32)
    for group in range(8):
        out[group] = total * (65536 ** -0.5)


def backward_body(tile, same, other, far, weight, input_grad):
    total = block_dot(tile, same, other) + far[...].astype(F32)
    input_grad[...] = dot(total.astype(BF16), weight[...], 1, 1)


def partner(rows):
    return lax.ppermute(rows, "zh", SWAP)


def after(value, *others):
    return lax.optimization_barrier((value,) + others)[0]


def over_y(message):
    return lax.all_to_all(message, "y", 0, 0)


def other_core(rows):
    return lax.ppermute(rows, "co", SWAP)


def local(features, weight, cotangent, block_values, block_codes, block_count):
    zh, core = lax.axis_index("zh"), lax.axis_index("co")
    hidden = features.shape[1]
    at = jnp.arange(hidden)
    group = 2 * (at // 256) + (at // 128 % 2 ^ core)
    source = 32 * (at // 4 % 32) + 4 * group + at % 4
    regroup = (jnp.arange(hidden)[:, None] == source[None, :]).astype(BF16)

    def shape(*dims, dtype=F32):
        return jax.ShapeDtypeStruct(dims, dtype)

    rows_f32, rows_bf16 = shape(128, hidden), shape(128, hidden, dtype=BF16)
    message_shape = shape(4, 128, hidden + 256, dtype=BF16)

    message, tile = pl.pallas_call(
        prepare_body,
        out_shape=(message_shape, shape(128, 1024, dtype=BF16)),
        in_specs=[SMEM] * 2 + [HBM] * 3,
        out_specs=(VMEM, VMEM),
        scratch_shapes=[
            pltpu.SMEM(block_codes.shape, jnp.int32),
            pltpu.VMEM(block_values.shape[1:], BF16),
            pltpu.SemaphoreType.DMA((6,)),
        ],
        compiler_params=pltpu.CompilerParams(vmem_limit_bytes=16 * 2**20),
    )(
        jnp.stack([zh, core]), block_count,
        *(
            pltpu.with_memory_space_constraint(a, pltpu.MemorySpace.HBM)
            for a in (block_codes, block_values, features)
        ),
    )
    same = over_y(message)
    other = other_core(same)
    far, mirror = call(first_far_body, (rows_bf16, shape(8, 128, 128, dtype=BF16)), same, other)
    far = partner(far)
    near = call(near_body, rows_f32, tile, same, other)
    output, message = call(
        forward_body, (rows_f32, message_shape), near, far, weight, cotangent, regroup
    )

    same = over_y(message)
    other = other_core(same)
    far, partial = pl.pallas_call(
        sums_body,
        out_shape=(
            pltpu.HBM(rows_bf16.shape, BF16), pltpu.HBM(rows_bf16.shape, BF16),
        ),
        in_specs=[VMEM] * 3,
        out_specs=(HBM, HBM),
        scratch_shapes=[
            pltpu.VMEM(rows_bf16.shape, BF16),
            pltpu.VMEM(rows_bf16.shape, BF16),
            pltpu.SemaphoreType.DMA((2,)),
        ],
        compiler_params=pltpu.CompilerParams(vmem_limit_bytes=16 * 2**20),
        cost_estimate=pl.CostEstimate(flops=1, bytes_accessed=1, transcendentals=0),
    )(mirror, same, other)
    part = lax.all_to_all(partial.reshape(4, 32, hidden), "x", 0, 0)
    far = partner(far)
    part = call(sum_x_body, shape(16, 4, hidden, dtype=BF16), part)
    part = lax.all_to_all(part, ("zh", "zl"), 0, 0)
    input_grad = call(backward_body, rows_f32, tile, same, other, far, weight, flops=10**11)
    part = call(sum_z_body, shape(8, 4, hidden), after(part, input_grad))
    part = lax.all_to_all(part, ("y", "co"), 0, 0)
    weight_grad = part.reshape(32, hidden)
    return output, input_grad, weight_grad


def solution(mesh):
    fine = Mesh(mesh.devices.reshape(SIZES), AXES)
    rows = P(AXES)
    return jax.shard_map(
        local,
        mesh=fine,
        in_specs=(rows, P(), rows, rows, rows, rows),
        out_specs=(rows, rows, P(("x", "zl"))),
        check_vma=False,
    )
```

```python
import jax
import jax.numpy as jnp
from jax import lax
from jax.experimental import pallas as pl
from jax.experimental.pallas import tpu as pltpu
from jax.sharding import Mesh, PartitionSpec as P

AXES = ("zh", "y", "co", "x", "zl")
SIZES = (2, 4, 2, 4, 8)
BF16, F32 = jnp.bfloat16, jnp.float32
SWAP = [(0, 1), (1, 0)]
VMEM = pl.BlockSpec(memory_space=pltpu.VMEM)
HBM = pl.BlockSpec(memory_space=pltpu.MemorySpace.HBM)
SMEM = pl.BlockSpec(memory_space=pltpu.SMEM)
COLS = slice(0, 1024)


def dot(a, b, over_a=1, over_b=0):
    return lax.dot_general(a, b, (((over_a,), (over_b,)), ((), ())), preferred_element_type=F32)


def call(body, outs, *args, flops=1):
    return pl.pallas_call(
        body,
        out_shape=outs,
        in_specs=[SMEM if a.dtype == jnp.int32 else VMEM for a in args],
        out_specs=jax.tree.map(lambda _: VMEM, outs),
        compiler_params=pltpu.CompilerParams(vmem_limit_bytes=16 * 2**20),
        cost_estimate=pl.CostEstimate(flops=flops, bytes_accessed=1, transcendentals=0),
    )(*args)


def block_dot(tile, same, other):
    total = 0.0
    for y in range(4):
        at = 128 * y
        total += dot(tile[:, at : at + 128], same[y, :, COLS])
        total += dot(tile[:, at + 512 : at + 640], other[y, :, COLS])
    return total


def near_body(tile, same, other, near):
    near[...] = block_dot(tile, same, other)


def forward_body(near, far, weight, cotangent, regroup, out, message):
    total = near[...] + far[...].astype(F32)
    high = total.astype(BF16)
    low = (total - high.astype(F32)).astype(BF16)
    summed = dot(high, weight[...]) + dot(low, weight[...])
    sigmoid = jax.nn.sigmoid(summed)
    out[...] = summed * sigmoid
    slope = cotangent[...].astype(F32) * sigmoid * (1.0 + summed * (1.0 - sigmoid))
    slope = slope.astype(BF16)
    factor = dot(high, regroup[...]).astype(BF16)
    for y in range(4):
        message[y, :, COLS] = slope
        message[y, :, 1024:1280] = factor[:, 256 * y : 256 * y + 256]


def prepare_body(place, count, codes_hbm, values_hbm, features, message, tile, codes, values, sems):
    copies = [
        pltpu.make_async_copy(codes_hbm, codes, sems.at[5]),
        pltpu.make_async_copy(values_hbm.at[0], values, sems.at[4]),
    ]
    for y in range(4):
        copies.append(pltpu.make_async_copy(features, message.at[y, :, COLS], sems.at[y]))
    for copy in copies:
        copy.start()
    tile[...] = jnp.zeros(tile.shape, BF16)
    for y in range(4):
        message[y, :, 1024:1280] = jnp.zeros((128, 256), BF16)
    copies[0].wait()
    copies[1].wait()

    def slot(k, carry):
        grid_row = lax.div(lax.rem(codes[0, k], 512), 32)
        y, other = lax.div(lax.rem(grid_row, 8), 2), lax.rem(grid_row + place[1], 2)
        own = lax.div(grid_row, 8) == place[0]

        @pl.when(own)
        def _():
            tile[:, pl.ds(pl.multiple_of(512 * other + 128 * y, 128), 128)] = values[k]

        @pl.when(jnp.logical_not(own))
        def _():
            message[y, :, pl.ds(pl.multiple_of(1024 + 128 * other, 128), 128)] = values[k]

        return carry

    lax.fori_loop(0, count[0], slot, 0)
    for copy in copies[2:]:
        copy.wait()


def grouped(same, other):
    total = 0.0
    for y in range(4):
        total += dot(same[y, :, 1024:1152], same[y, :, COLS], 0, 0)
        total += dot(other[y, :, 1152:1280], other[y, :, COLS], 0, 0)
    return total


def first_far_body(same, other, far, mirror):
    far[...] = grouped(same, other).astype(BF16)
    for y in range(4):
        mirror[y] = same[y, :, 1024:1152]
        mirror[y + 4] = other[y, :, 1152:1280]


def sums_body(mirror, same, other, far_hbm, partial_hbm, far, partial, sems):
    far_here = 0.0
    for y in range(4):
        far_here += dot(mirror[y], same[y, :, COLS], 0, 0)
        far_here += dot(mirror[y + 4], other[y, :, COLS], 0, 0)
    far[...] = far_here.astype(BF16)
    far_copy = pltpu.make_async_copy(far, far_hbm, sems.at[0])
    far_copy.start()
    partial[...] = grouped(same, other)
    partial_copy = pltpu.make_async_copy(partial, partial_hbm, sems.at[1])
    partial_copy.start()
    far_copy.wait()
    partial_copy.wait()


def sum_x_body(pieces, out):
    total = pieces[0] + pieces[1] + pieces[2] + pieces[3]
    for z in range(8):
        rows = total[4 * z : 4 * z + 4].astype(BF16)
        out[z] = rows
        out[z + 8] = rows


def sum_z_body(pieces, out):
    total = pieces[0].astype(F32)
    for z in range(1, 16):
        total += pieces[z].astype(F32)
    for group in range(8):
        out[group] = total * (65536 ** -0.5)


def backward_body(tile, same, other, far, weight, input_grad):
    total = block_dot(tile, same, other) + far[...].astype(F32)
    input_grad[...] = dot(total.astype(BF16), weight[...], 1, 1)


def partner(rows):
    return lax.ppermute(rows, "zh", SWAP)


def partner_by_fours(rows):
    pairs = []
    for z in range(16):
        for core in range(2):
            to = (z + (4 if core == 0 else -4)) % 16
            pairs.append((z // 8 * 16 + core * 8 + z % 8, to // 8 * 16 + core * 8 + to % 8))
    for _ in range(2):
        rows = lax.ppermute(rows, ("zh", "co", "zl"), pairs)
    return rows


def after(value, *others):
    return lax.optimization_barrier((value,) + others)[0]


def over_y(message):
    return lax.all_to_all(message, "y", 0, 0)


def other_core(rows):
    return lax.ppermute(rows, "co", SWAP)


def local(features, weight, cotangent, block_values, block_codes, block_count):
    zh, core = lax.axis_index("zh"), lax.axis_index("co")
    hidden = features.shape[1]
    at = jnp.arange(hidden)
    group = 2 * (at // 256) + (at // 128 % 2 ^ core)
    source = 32 * (at // 4 % 32) + 4 * group + at % 4
    regroup = (jnp.arange(hidden)[:, None] == source[None, :]).astype(BF16)

    def shape(*dims, dtype=F32):
        return jax.ShapeDtypeStruct(dims, dtype)

    rows_f32, rows_bf16 = shape(128, hidden), shape(128, hidden, dtype=BF16)
    message_shape = shape(4, 128, hidden + 256, dtype=BF16)

    message, tile = pl.pallas_call(
        prepare_body,
        out_shape=(message_shape, shape(128, 1024, dtype=BF16)),
        in_specs=[SMEM] * 2 + [HBM] * 3,
        out_specs=(VMEM, VMEM),
        scratch_shapes=[
            pltpu.SMEM(block_codes.shape, jnp.int32),
            pltpu.VMEM(block_values.shape[1:], BF16),
            pltpu.SemaphoreType.DMA((6,)),
        ],
        compiler_params=pltpu.CompilerParams(vmem_limit_bytes=16 * 2**20),
    )(
        jnp.stack([zh, core]), block_count,
        *(
            pltpu.with_memory_space_constraint(a, pltpu.MemorySpace.HBM)
            for a in (block_codes, block_values, features)
        ),
    )
    same = over_y(message)
    other = other_core(same)
    far, mirror = call(first_far_body, (rows_bf16, shape(8, 128, 128, dtype=BF16)), same, other)
    far = partner_by_fours(far)
    near = call(near_body, rows_f32, tile, same, other)
    output, message = call(
        forward_body, (rows_f32, message_shape), near, far, weight, cotangent, regroup
    )

    same = over_y(message)
    other = other_core(same)
    far, partial = pl.pallas_call(
        sums_body,
        out_shape=(
            pltpu.HBM(rows_bf16.shape, BF16), pltpu.HBM(rows_f32.shape, F32),
        ),
        in_specs=[VMEM] * 3,
        out_specs=(HBM, HBM),
        scratch_shapes=[
            pltpu.VMEM(rows_bf16.shape, BF16),
            pltpu.VMEM(rows_f32.shape, F32),
            pltpu.SemaphoreType.DMA((2,)),
        ],
        compiler_params=pltpu.CompilerParams(vmem_limit_bytes=16 * 2**20),
        cost_estimate=pl.CostEstimate(flops=1, bytes_accessed=1, transcendentals=0),
    )(mirror, same, other)
    part = lax.all_to_all(partial.reshape(4, 32, hidden), "x", 0, 0)
    far = partner(far)
    part = call(sum_x_body, shape(16, 4, hidden, dtype=BF16), part)
    part = lax.all_to_all(part, ("zh", "zl"), 0, 0)
    input_grad = call(backward_body, rows_f32, tile, same, other, far, weight, flops=10**11)
    part = call(sum_z_body, shape(8, 4, hidden), after(part, input_grad))
    part = lax.all_to_all(part, ("y", "co"), 0, 0)
    weight_grad = part.reshape(32, hidden)
    return output, input_grad, weight_grad


def solution(mesh):
    fine = Mesh(mesh.devices.reshape(SIZES), AXES)
    rows = P(AXES)
    return jax.shard_map(
        local,
        mesh=fine,
        in_specs=(rows, P(), rows, rows, rows, rows),
        out_specs=(rows, rows, P(("x", "zl"))),
        check_vma=False,
    )
```

```python
import jax
import jax.numpy as jnp
from jax import lax
from jax.experimental import pallas as pl
from jax.experimental.pallas import tpu as pltpu
from jax.sharding import Mesh, PartitionSpec as P

AXES = ("zh", "y", "co", "x", "zl")
SIZES = (2, 4, 2, 4, 8)
BF16, F32 = jnp.bfloat16, jnp.float32
SWAP = [(0, 1), (1, 0)]
VMEM = pl.BlockSpec(memory_space=pltpu.VMEM)
HBM = pl.BlockSpec(memory_space=pltpu.MemorySpace.HBM)
SMEM = pl.BlockSpec(memory_space=pltpu.SMEM)
COLS = slice(0, 1024)


def dot(a, b, over_a=1, over_b=0):
    return lax.dot_general(a, b, (((over_a,), (over_b,)), ((), ())), preferred_element_type=F32)


def call(body, outs, *args, flops=1):
    return pl.pallas_call(
        body,
        out_shape=outs,
        in_specs=[SMEM if a.dtype == jnp.int32 else VMEM for a in args],
        out_specs=jax.tree.map(lambda _: VMEM, outs),
        compiler_params=pltpu.CompilerParams(vmem_limit_bytes=16 * 2**20),
        cost_estimate=pl.CostEstimate(flops=flops, bytes_accessed=1, transcendentals=0),
    )(*args)


def block_dot(tile, same, other):
    total = 0.0
    for y in range(4):
        at = 128 * y
        total += dot(tile[:, at : at + 128], same[y, :, COLS])
        total += dot(tile[:, at + 512 : at + 640], other[y, :, COLS])
    return total


def near_body(tile, same, other, near):
    near[...] = block_dot(tile, same, other)


def forward_body(near, far, weight, cotangent, regroup, out, message):
    total = near[...] + far[...].astype(F32)
    high = total.astype(BF16)
    low = (total - high.astype(F32)).astype(BF16)
    summed = dot(high, weight[...]) + dot(low, weight[...])
    sigmoid = jax.nn.sigmoid(summed)
    out[...] = summed * sigmoid
    slope = cotangent[...].astype(F32) * sigmoid * (1.0 + summed * (1.0 - sigmoid))
    slope = slope.astype(BF16)
    factor = dot(high, regroup[...]).astype(BF16)
    for y in range(4):
        message[y, :, COLS] = slope
        message[y, :, 1024:1280] = factor[:, 256 * y : 256 * y + 256]


def prepare_body(count, codes_hbm, values_hbm, features, message, tile, codes, values, sems):
    copies = [
        pltpu.make_async_copy(codes_hbm, codes, sems.at[5]),
        pltpu.make_async_copy(values_hbm.at[0], values, sems.at[4]),
    ]
    for y in range(4):
        copies.append(pltpu.make_async_copy(features, message.at[y, :, COLS], sems.at[y]))
    for copy in copies:
        copy.start()
    tile[...] = jnp.zeros(tile.shape, BF16)
    for y in range(4):
        message[y, :, 1024:1280] = jnp.zeros((128, 256), BF16)
    zh, core = lax.axis_index("zh"), lax.axis_index("co")
    copies[0].wait()
    copies[1].wait()

    def slot(k, carry):
        grid_row = lax.div(lax.rem(codes[0, k], 512), 32)
        y, other = lax.div(lax.rem(grid_row, 8), 2), lax.rem(grid_row + core, 2)
        own = lax.div(grid_row, 8) == zh

        @pl.when(own)
        def _():
            tile[:, pl.ds(pl.multiple_of(512 * other + 128 * y, 128), 128)] = values[k]

        @pl.when(jnp.logical_not(own))
        def _():
            message[y, :, pl.ds(pl.multiple_of(1024 + 128 * other, 128), 128)] = values[k]

        return carry

    lax.fori_loop(0, count[0], slot, 0)
    for copy in copies[2:]:
        copy.wait()


def grouped(same, other):
    total = 0.0
    for y in range(4):
        total += dot(same[y, :, 1024:1152], same[y, :, COLS], 0, 0)
        total += dot(other[y, :, 1152:1280], other[y, :, COLS], 0, 0)
    return total


def first_far_body(same, other, far, mirror):
    far[...] = grouped(same, other).astype(BF16)
    for y in range(4):
        mirror[y] = same[y, :, 1024:1152]
        mirror[y + 4] = other[y, :, 1152:1280]


def sums_body(mirror, same, other, far_hbm, partial_hbm, far, partial, sems):
    far_here = 0.0
    for y in range(4):
        far_here += dot(mirror[y], same[y, :, COLS], 0, 0)
        far_here += dot(mirror[y + 4], other[y, :, COLS], 0, 0)
    far[...] = far_here.astype(BF16)
    far_copy = pltpu.make_async_copy(far, far_hbm, sems.at[0])
    far_copy.start()
    partial[...] = grouped(same, other)
    partial_copy = pltpu.make_async_copy(partial, partial_hbm, sems.at[1])
    partial_copy.start()
    far_copy.wait()
    partial_copy.wait()


def sum_x_body(pieces, out):
    total = pieces[0] + pieces[1] + pieces[2] + pieces[3]
    for z in range(8):
        rows = total[4 * z : 4 * z + 4].astype(BF16)
        out[z] = rows
        out[z + 8] = rows


def sum_z_body(pieces, out):
    total = pieces[0].astype(F32)
    for z in range(1, 16):
        total += pieces[z].astype(F32)
    for group in range(8):
        out[group] = total * (65536 ** -0.5)


def backward_body(tile, same, other, far, weight, input_grad):
    total = block_dot(tile, same, other) + far[...].astype(F32)
    input_grad[...] = dot(total.astype(BF16), weight[...], 1, 1)


def partner(rows):
    return lax.ppermute(rows, "zh", SWAP)


def after(value, *others):
    return lax.optimization_barrier((value,) + others)[0]


def over_y(message):
    return lax.all_to_all(message, "y", 0, 0)


def other_core(rows):
    return lax.ppermute(rows, "co", SWAP)


def local(features, weight, cotangent, block_values, block_codes, block_count):
    core = lax.axis_index("co")
    hidden = features.shape[1]
    at = jnp.arange(hidden)
    group = 2 * (at // 256) + (at // 128 % 2 ^ core)
    source = 32 * (at // 4 % 32) + 4 * group + at % 4
    regroup = (jnp.arange(hidden)[:, None] == source[None, :]).astype(BF16)

    def shape(*dims, dtype=F32):
        return jax.ShapeDtypeStruct(dims, dtype)

    rows_f32, rows_bf16 = shape(128, hidden), shape(128, hidden, dtype=BF16)
    message_shape = shape(4, 128, hidden + 256, dtype=BF16)

    message, tile = pl.pallas_call(
        prepare_body,
        out_shape=(message_shape, shape(128, 1024, dtype=BF16)),
        in_specs=[SMEM] + [HBM] * 3,
        out_specs=(VMEM, VMEM),
        scratch_shapes=[
            pltpu.SMEM(block_codes.shape, jnp.int32),
            pltpu.VMEM(block_values.shape[1:], BF16),
            pltpu.SemaphoreType.DMA((6,)),
        ],
        compiler_params=pltpu.CompilerParams(vmem_limit_bytes=16 * 2**20),
    )(
        block_count,
        *(
            pltpu.with_memory_space_constraint(a, pltpu.MemorySpace.HBM)
            for a in (block_codes, block_values, features)
        ),
    )
    same = over_y(message)
    other = other_core(same)
    far, mirror = call(first_far_body, (rows_bf16, shape(8, 128, 128, dtype=BF16)), same, other)
    far = partner(far)
    near = call(near_body, rows_f32, tile, same, other)
    output, message = call(
        forward_body, (rows_f32, message_shape), near, far, weight, cotangent, regroup
    )

    same = over_y(message)
    other = other_core(same)
    far, partial = pl.pallas_call(
        sums_body,
        out_shape=(
            pltpu.HBM(rows_bf16.shape, BF16), pltpu.HBM(rows_f32.shape, F32),
        ),
        in_specs=[VMEM] * 3,
        out_specs=(HBM, HBM),
        scratch_shapes=[
            pltpu.VMEM(rows_bf16.shape, BF16),
            pltpu.VMEM(rows_f32.shape, F32),
            pltpu.SemaphoreType.DMA((2,)),
        ],
        compiler_params=pltpu.CompilerParams(vmem_limit_bytes=16 * 2**20),
        cost_estimate=pl.CostEstimate(flops=1, bytes_accessed=1, transcendentals=0),
    )(mirror, same, other)
    part = lax.all_to_all(partial.reshape(4, 32, hidden), "x", 0, 0)
    far = partner(far)
    part = call(sum_x_body, shape(16, 4, hidden, dtype=BF16), part)
    part = lax.all_to_all(part, ("zh", "zl"), 0, 0)
    input_grad = call(backward_body, rows_f32, tile, same, other, far, weight, flops=10**11)
    part = call(sum_z_body, shape(8, 4, hidden), after(part, input_grad))
    part = lax.all_to_all(part, ("y", "co"), 0, 0)
    weight_grad = part.reshape(32, hidden)
    return output, input_grad, weight_grad


def solution(mesh):
    fine = Mesh(mesh.devices.reshape(SIZES), AXES)
    rows = P(AXES)
    return jax.shard_map(
        local,
        mesh=fine,
        in_specs=(rows, P(), rows, rows, rows, rows),
        out_specs=(rows, rows, P(("x", "zl"))),
        check_vma=False,
    )
```
